256 devices in a mesh: dp: 2 (over z_hi), layer: 4 (over y), feat: 32 (over z_lo, x, core).
Axes of the slice: x: 4, y: 4, z: 8 (z_hi: 2, z_lo: 4; z = z_hi * 4 + z_lo), core: 2. Of those that a mesh axis runs over, the one named last changes fastest.
Arguments:
- resid: bfloat16 [4, 1024, 2304], P('layer', 'dp'), may hold values from -6 to 6
- enc_weight: bfloat16 [4, 2304, 16384], P('layer', None, 'feat'), may hold values from -0.125 to 0.125
- enc_bias: float32 [4, 16384], P('layer', 'feat'), may hold values from -3 to 3
- dec_weight: bfloat16 [4, 4, 16384, 2304], P('layer', None, 'feat', 'dp'), may hold values from -0.09375 to 0.09375
- dec_bias: float32 [4, 2304], P('layer', ('dp', 'feat')), may hold values from -3 to 3
- lengths: int32 [8], P('dp'), may hold values from 32 to 128, as said below
Outputs:
- recon: bfloat16 [4, 1024, 2304], P('layer', None, ('dp', 'feat'))
The draws below stay inside these ranges and needn't reach their ends.
Inputs may be any that keep to these rules, and one draw needn't show every extreme that they name: `lengths`: the first sequence has length 128.
All inputs are finite; a program needn't handle non-finite values.
Results may differ from the reference program's by a relative error of at most 0.0047.
Values may be sent and summed in bfloat16 or wider, within the bound.
No kernel may reach another device: no remote copies, remote signals or barrier semaphores. Data moves between devices by JAX's collectives and lax.ppermute only.
A program may use at most 64 MiB of HBM per device.

```python
import jax
import jax.numpy as jnp

D = 2304
FEATS = 16384
LAYERS = 4
SEQ = 128
ROWS = 1024
NSEQ = 8


def draw_lengths(key, part):
    lowest = max(1, SEQ // 4)
    drawn = jax.random.randint(key, (NSEQ,), lowest, SEQ + 1).astype(jnp.int32)
    return drawn.at[0].set(SEQ)


def spiked(entries, key, source, target, parts, factor):
    owner, partner = [(jnp.arange(entries.shape[dim]) // (entries.shape[dim] // parts)).reshape([-1 if axis == dim else 1 for axis in range(entries.ndim)]) for dim in (source, target)]
    chosen = jax.random.permutation(key, parts)[partner]
    strong = (owner == chosen) | (owner == (partner + parts // 2) % parts)
    return jnp.where(strong, factor * entries, entries)


def steps_of(rng, shape, shards, smallest, largest):
    level = 1.0
    for axis_at, parts in shards:
        heights = jax.random.uniform(jax.random.fold_in(jax.random.fold_in(rng, 6), axis_at), (parts,), jnp.float32, smallest / len(shards), largest / len(shards))
        level = level * jnp.repeat(jnp.exp(heights), shape[axis_at] // parts).reshape((-1,) + (1,) * (len(shape) - 1 - axis_at))
    return level


def bell_draw(stream_key, dims, deviation, reach, shards=(), held_as=jnp.bfloat16):
    loudness = steps_of(stream_key, dims, shards, -0.22, 0.18) if shards else 1.0
    entries = jax.random.normal(stream_key, dims, jnp.float32) * deviation * loudness
    return jnp.minimum(jnp.maximum(entries, -reach), reach).astype(held_as)


def noise_with(key, dims, scale, reach, shards, heavy, dtype=jnp.bfloat16):
    result = scale * jax.random.normal(key, dims, jnp.float32)
    if shards:
        result = result * steps_of(key, dims, shards, -0.22, 0.18)
    return jnp.clip(spiked(result, jax.random.fold_in(key, 3), *heavy), -reach, reach).astype(dtype)


def setup_inputs(seed: int = 0) -> dict:
    arg_keys = jax.random.split(jax.random.key(seed), 7)
    return {
        "resid": bell_draw(arg_keys[0], (LAYERS, ROWS, D), 1.0, 6.0, ((0, 4), (1, 2))),
        "enc_weight": bell_draw(arg_keys[1], (LAYERS, D, FEATS), D ** -0.5, 0.125, ((0, 4), (2, 32))),
        "enc_bias": bell_draw(arg_keys[2], (LAYERS, FEATS), 0.5, 3.0, ((0, 4), (1, 32)), jnp.float32),
        "dec_weight": noise_with(arg_keys[3], (LAYERS, LAYERS, FEATS, D), FEATS ** -0.5, 0.09375, ((0, 4), (2, 32), (3, 2)), (2, 3, 32, 2.75)),
        "dec_bias": bell_draw(arg_keys[4], (LAYERS, D), 0.5, 3.0, ((0, 4), (1, 64)), jnp.float32),
        "lengths": draw_lengths(jax.random.fold_in(arg_keys[6], 71), 0),
    }


def reference(resid, enc_weight, enc_bias, dec_weight, dec_bias, lengths):
    valid = (jnp.arange(SEQ)[None, :] < lengths[:, None]).reshape(-1).astype(jnp.float32)
    acts = []
    for source in range(LAYERS):
        pre = jnp.dot(resid[source], enc_weight[source], preferred_element_type=jnp.float32) + enc_bias[source]
        acts.append((jax.nn.relu(pre) * valid[:, None]).astype(jnp.bfloat16))
    outputs = []
    for target in range(LAYERS):
        total = jnp.zeros((resid.shape[1], resid.shape[2]), jnp.float32)
        for source in range(target + 1):
            total = total + jnp.dot(acts[source], dec_weight[target, source], preferred_element_type=jnp.float32)
        outputs.append((total + dec_bias[target]).astype(jnp.bfloat16))
    return jnp.stack(outputs)
```

```python
import jax
import jax.numpy as jnp
from jax import lax
from jax.sharding import PartitionSpec as P

SEQ = 128
BF = jnp.bfloat16
F32 = jnp.float32


def feat_groups():
    at = lambda z, x, c: z * 8 + x * 2 + c
    along_x = [[at(z, x, c) for x in range(4)] for z in range(4) for c in range(2)]
    along_z = [[at(z, x, c) for z in range(4)] for x in range(4) for c in range(2)]
    return along_x, along_z


def layer_exchange(acts, target):
    half = acts.shape[0] // 2
    up = lax.ppermute(acts, "layer", [(0, 1), (1, 2), (2, 3)])
    down = lax.ppermute(acts, "layer", [(0, 3), (1, 0)])
    far_up = lax.ppermute(up[:half], "layer", [(1, 2), (2, 3)])
    far_down = lax.ppermute(down[half:], "layer", [(3, 2), (0, 3)])
    return up, jnp.where(target == 3, down, 0), jnp.concatenate([far_up, far_down])


def partial_recon(blocks, decoders, target):
    total = None
    for back, block in blocks:
        matrix = lax.dynamic_index_in_dim(decoders, jnp.maximum(target - back, 0), 0, keepdims=False)
        halves = block.reshape(2, block.shape[0] // 2, block.shape[1])
        term = jnp.einsum("fc,grf->gcr", matrix, halves, preferred_element_type=F32)
        total = term if total is None else total + term
    return total


def reduce_features(total, core):
    along_x, along_z = feat_groups()
    partner = [(i, i ^ 1) for i in range(32)]
    away = lax.dynamic_index_in_dim(total, 1 - core, 0, keepdims=False).astype(BF)
    kept = lax.dynamic_index_in_dim(total, core, 0, keepdims=False)
    chip = kept + lax.ppermute(away, "feat", partner).astype(F32)
    rows = chip.shape[1]
    pieces = chip.astype(BF).reshape(4, 4, 72, rows).transpose(1, 0, 2, 3)
    pieces = lax.all_to_all(pieces, "feat", 0, 0, tiled=True, axis_index_groups=along_x)
    pieces = pieces.astype(F32).sum(0).astype(BF)
    pieces = lax.all_to_all(pieces, "feat", 0, 0, tiled=True, axis_index_groups=along_z)
    return pieces.astype(F32).sum(0)


def per_device(resid, enc_weight, enc_bias, dec_weight, dec_bias, lengths):
    target = lax.axis_index("layer")
    core = lax.axis_index("feat") % 2
    valid = (jnp.arange(SEQ)[None, :] < lengths[:, None]).reshape(-1).astype(F32)
    pre = jnp.dot(resid[0], enc_weight[0], preferred_element_type=F32) + enc_bias[0]
    own = (jax.nn.relu(pre) * valid[:, None]).astype(BF)
    other = lax.ppermute(own, "dp", [(0, 1), (1, 0)])
    decoders = dec_weight[0]
    sums = []
    for acts in (own, other):
        one, three, two = layer_exchange(acts, target)
        blocks = [(0, acts), (1, one), (3, three), (2, two)]
        sums.append(reduce_features(partial_recon(blocks, decoders, target), core))
    both = jnp.stack(sums)
    partner = [(i, i ^ 1) for i in range(32)]
    low, high = both[:, :36], both[:, 36:]
    kept = jnp.where(core == 0, low, high)
    came = lax.ppermute(jnp.where(core == 0, high, low), "feat", partner)
    halves = jnp.where(core == 0, jnp.concatenate([kept, came], 2), jnp.concatenate([came, kept], 2))
    halves = jnp.where(lax.axis_index("dp") == 0, halves, halves[::-1])
    out = jnp.concatenate([halves[0], halves[1]], 1) + dec_bias[0][:, None]
    return out.T.astype(BF)[None]


def solution(mesh):
    in_specs = (
        P("layer", "dp", None),
        P("layer", None, "feat"),
        P("layer", "feat"),
        P("layer", None, "feat", "dp"),
        P("layer", ("dp", "feat")),
        P("dp"),
    )
    out_specs = P("layer", None, ("dp", "feat"))
    return jax.shard_map(
        per_device, mesh=mesh, in_specs=in_specs, out_specs=out_specs, check_vma=False
    )
```

```python
import functools

import jax
import jax.numpy as jnp
from jax import lax
from jax.experimental import pallas as pl
from jax.experimental.pallas import tpu as pltpu
from jax.sharding import PartitionSpec as P

SEQ = 128
BF = jnp.bfloat16
F32 = jnp.float32

NX, NZ = 4, 4
PARTNER = [(i, i ^ 1) for i in range(32)]


def feat_at(z, x, c):
    return z * 8 + x * 2 + c


def x_pairs(by):
    return [
        (feat_at(z, x, c), feat_at(z, (x + by) % NX, c))
        for z in range(NZ) for x in range(NX) for c in range(2)
    ]


ZC_GROUPS = [[feat_at(z, x, c) for z in range(NZ) for c in range(2)] for x in range(NX)]


def whole(shape):
    return pl.BlockSpec(shape, lambda *_: (0,) * len(shape))


def encode_kernel(at_ref, len_ref, resid_ref, weight_ref, bias_ref, keep_ref, send_ref, total):
    step = pl.program_id(0)
    term = jnp.dot(resid_ref[0], weight_ref[0], preferred_element_type=F32)

    @pl.when(step == 0)
    def _():
        total[...] = term

    @pl.when(step > 0)
    def _():
        total[...] += term

    @pl.when(step == pl.num_programs(0) - 1)
    def _():
        core = at_ref[0]
        for ref, half in ((keep_ref, core), (send_ref, 1 - core)):
            for s in range(2):
                seq = half * 2 + s
                pre = total[pl.ds(pl.multiple_of(seq * SEQ, SEQ), SEQ), :] + bias_ref[...]
                row = lax.broadcasted_iota(jnp.int32, pre.shape, 0)
                acts = jnp.where(row < len_ref[seq], jnp.maximum(pre, 0.0), 0.0)
                ref[s * SEQ : (s + 1) * SEQ, :] = acts.astype(BF)


def encode(at, lengths, resid, weight, bias):
    rows, depth = resid.shape[1:]
    feats = weight.shape[2]
    tile = 384
    half = jax.ShapeDtypeStruct((rows // 2, feats), BF)
    return pl.pallas_call(
        encode_kernel,
        out_shape=(half, half),
        grid_spec=pltpu.PrefetchScalarGridSpec(
            num_scalar_prefetch=2,
            grid=(depth // tile,),
            in_specs=[
                pl.BlockSpec((1, rows, tile), lambda k, *_: (0, 0, k)),
                pl.BlockSpec((1, tile, feats), lambda k, *_: (0, k, 0)),
                whole((1, feats)),
            ],
            out_specs=(whole(half.shape), whole(half.shape)),
            scratch_shapes=[pltpu.VMEM((rows, feats), F32)],
        ),
        cost_estimate=pl.CostEstimate(
            flops=2 * rows * depth * feats, bytes_accessed=2 * depth * (rows + feats), transcendentals=0
        ),
        name="encode",
    )(at, lengths, resid, weight, bias)


TILE = 384


def weight_specs(back):
    at = lambda n, at_ref: (0, jnp.maximum(at_ref[1] - back, 0), 0, n)
    return [pl.BlockSpec((1, 1, 512, TILE), at)] * 2


def add_terms(backs, at_ref, refs, total_ref):
    for i, back in enumerate(backs):
        mine, theirs, w_mine, w_theirs = refs[4 * i : 4 * i + 4]

        def add(mine=mine, theirs=theirs, w_mine=w_mine, w_theirs=w_theirs):
            term = jnp.dot(mine[...], w_mine[0, 0], preferred_element_type=F32)
            term += jnp.dot(theirs[...], w_theirs[0, 0], preferred_element_type=F32)
            total_ref[...] += term

        if back:
            pl.when(at_ref[1] >= back)(add)
        else:
            add()


def partial_kernel(backs, has_base, at_ref, *refs):
    total_ref = refs[-1]
    if has_base:
        total_ref[...] = refs[0][...]
        refs = refs[1:]
    else:
        total_ref[...] = jnp.zeros_like(total_ref)
    add_terms(backs, at_ref, refs, total_ref)


def term_operands(terms, w_mine, w_theirs):
    specs, operands = [], []
    for back, (mine, theirs) in terms:
        for array, index in (mine, theirs):
            if array.ndim == 3:
                specs.append(pl.BlockSpec((pl.Squeezed(), *array.shape[1:]), lambda n, *_, i=index: (i, 0, 0)))
            else:
                specs.append(whole(array.shape))
            operands.append(array)
        specs += weight_specs(back)
        operands += [w_mine, w_theirs]
    return specs, operands


def cost(terms, rows):
    n = 2 * len(terms)
    return pl.CostEstimate(
        flops=2 * n * rows * 512 * 1152, bytes_accessed=n * 512 * 1152 * 2 + rows * 1152 * 8, transcendentals=0
    )


def partial(at, terms, w_mine, w_theirs, base=None):
    rows, cols = terms[0][1][0][0].shape[-2], w_mine.shape[3]
    specs, operands = term_operands(terms, w_mine, w_theirs)
    tile = pl.BlockSpec((rows, TILE), lambda n, *_: (0, n))
    if base is not None:
        specs, operands = [tile] + specs, [base] + operands
    return pl.pallas_call(
        functools.partial(partial_kernel, [b for b, _ in terms], base is not None),
        out_shape=jax.ShapeDtypeStruct((rows, cols), F32),
        grid_spec=pltpu.PrefetchScalarGridSpec(
            num_scalar_prefetch=1, grid=(cols // TILE,), in_specs=specs, out_specs=tile
        ),
        cost_estimate=cost(terms, rows),
        name="partial",
    )(at, *operands)


def last_kernel(backs, at_ref, base_ref, *refs):
    turned, total_ref = refs[-2:]
    self_ref, *away = refs[-6:-2]
    n = pl.program_id(0)
    total_ref[...] = base_ref[...]
    add_terms(backs, at_ref, refs, total_ref)
    turned[pl.ds(pl.multiple_of(n * TILE, TILE), TILE), :] = total_ref[...].T

    @pl.when(n == pl.num_programs(0) - 1)
    def _():
        for by in range(NX):
            owner = lax.rem(at_ref[2] + by, NX)
            for z in range(NZ):
                piece = turned[pl.ds(pl.multiple_of((z * NX + owner) * 72, 8), 72), :]
                if by == 0:
                    self_ref[z] = piece
                else:
                    away[by - 1][z] = piece.astype(BF)


def last(at, base, terms, w_mine, w_theirs):
    rows, cols = base.shape
    specs, operands = term_operands(terms, w_mine, w_theirs)
    tile = pl.BlockSpec((rows, TILE), lambda n, *_: (0, n))
    piece = (NZ, cols // (NX * NZ), rows)
    return pl.pallas_call(
        functools.partial(last_kernel, [b for b, _ in terms]),
        out_shape=[jax.ShapeDtypeStruct(piece, F32)] + [jax.ShapeDtypeStruct(piece, BF)] * 3,
        grid_spec=pltpu.PrefetchScalarGridSpec(
            num_scalar_prefetch=1,
            grid=(cols // TILE,),
            in_specs=[tile] + specs,
            out_specs=[whole(piece)] * 4,
            scratch_shapes=[pltpu.VMEM((cols, rows), F32), pltpu.VMEM((rows, TILE), F32)],
        ),
        cost_estimate=cost(terms, rows),
        name="last",
    )(at, base, *operands)


def x_sum_kernel(self_ref, a_ref, b_ref, c_ref, out_ref):
    for z in range(NZ):
        total = self_ref[z] + a_ref[z].astype(F32) + b_ref[z].astype(F32) + c_ref[z].astype(F32)
        total = total.astype(BF)
        out_ref[2 * z] = total[:36]
        out_ref[2 * z + 1] = total[36:]


def reduce_features(pieces):
    kept, *away = pieces
    came = [lax.ppermute(piece, "feat", x_pairs(by + 1)) for by, piece in enumerate(away)]
    rows = kept.shape[2]
    chips = pl.pallas_call(
        x_sum_kernel, out_shape=jax.ShapeDtypeStruct((2 * NZ, 36, rows), BF), name="x_sum"
    )(kept, *came)
    return lax.all_to_all(chips, "feat", 0, 0, tiled=True, axis_index_groups=ZC_GROUPS)


def final_kernel(at_ref, own_ref, other_ref, bias_ref, out_ref):
    for ref, flip in ((own_ref, 0), (other_ref, 1)):
        for c in range(2):
            total = bias_ref[...]
            for z in range(NZ):
                total = total + ref[2 * z + c].astype(F32)
            total = total.astype(BF)
            for dp in range(2):

                @pl.when(at_ref[3] == dp)
                def _(total=total, start=((dp + flip) % 2) * 512 + c * 256):
                    out_ref[:, start : start + 256] = total


def finish(at, own, other, bias):
    return pl.pallas_call(
        final_kernel,
        out_shape=jax.ShapeDtypeStruct((36, 1024), BF),
        grid_spec=pltpu.PrefetchScalarGridSpec(
            num_scalar_prefetch=1,
            grid=(1,),
            in_specs=[whole(own.shape), whole(other.shape), whole(bias.shape)],
            out_specs=whole((36, 1024)),
        ),
        name="finish",
    )(at, own, other, bias)


def per_device(resid, enc_weight, enc_bias, dec_weight, dec_bias, lengths):
    target, feat, dp = lax.axis_index("layer"), lax.axis_index("feat"), lax.axis_index("dp")
    at = jnp.stack([feat % 2, target, feat // 2 % NX, dp]).astype(jnp.int32)
    theirs_w = lax.ppermute(dec_weight, "feat", PARTNER)
    keep, send = encode(at, lengths, resid, enc_weight, enc_bias)
    across = lambda flip: [(d * 32 + f, (1 - d) * 32 + (f ^ flip)) for d in range(2) for f in range(32)]
    other_mine = lax.ppermute(keep, ("dp", "feat"), across(0))
    other_theirs = lax.ppermute(send, ("dp", "feat"), across(1))
    own_theirs = lax.ppermute(send, "feat", PARTNER)
    results = []
    for mine, theirs in ((keep, own_theirs), (other_mine, other_theirs)):
        acts = jnp.stack([mine, theirs])
        up = lax.ppermute(acts, "layer", [(0, 1), (1, 2), (2, 3)])
        down = lax.ppermute(acts, "layer", [(0, 3), (1, 0)])
        far_up = lax.ppermute(up[0], "layer", [(1, 2), (2, 3)])
        far_down = lax.ppermute(down[1], "layer", [(3, 2), (0, 3)])
        total = partial(at, [(0, ((acts, 0), (acts, 1)))], dec_weight, theirs_w)
        total = partial(
            at,
            [(1, ((up, 0), (up, 1))), (3, ((down, 0), (down, 1)))],
            dec_weight, theirs_w, total,
        )
        pieces = last(at, total, [(2, ((far_up, 0), (far_down, 0)))], dec_weight, theirs_w)
        results.append(reduce_features(pieces))
    out = finish(at, *results, dec_bias.reshape(36, 1))
    return out.T[None]


def solution(mesh):
    in_specs = (
        P("layer", "dp", None),
        P("layer", None, "feat"),
        P("layer", "feat"),
        P("layer", None, "feat", "dp"),
        P("layer", ("dp", "feat")),
        P("dp"),
    )
    out_specs = P("layer", None, ("dp", "feat"))
    return jax.shard_map(
        per_device, mesh=mesh, in_specs=in_specs, out_specs=out_specs, check_vma=False
    )
```

```python
import functools

import jax
import jax.numpy as jnp
from jax import lax
from jax.experimental import pallas as pl
from jax.experimental.pallas import tpu as pltpu
from jax.sharding import PartitionSpec as P


SEQ = 128
BF = jnp.bfloat16
F32 = jnp.float32

NX, NZ = 4, 4
PARTNER = [(i, i ^ 1) for i in range(32)]


def feat_at(z, x, c):
    return z * 8 + x * 2 + c


def x_pairs(by):
    return [
        (feat_at(z, x, c), feat_at(z, (x + by) % NX, c))
        for z in range(NZ) for x in range(NX) for c in range(2)
    ]


ZC_GROUPS = [[feat_at(z, x, c) for z in range(NZ) for c in range(2)] for x in range(NX)]


IN_VMEM = pl.BlockSpec(memory_space=pltpu.VMEM)
IN_SMEM = pl.BlockSpec(memory_space=pltpu.SMEM)
MIB = 1 << 20


def call(kernel, out_shape, operands, grant, scratch=(), flops=0):
    single = not isinstance(out_shape, (list, tuple))
    moved = sum(a.size * a.dtype.itemsize for a in operands)
    return pl.pallas_call(
        kernel,
        out_shape=out_shape,
        in_specs=[IN_SMEM] + [IN_VMEM] * (len(operands) - 1),
        out_specs=IN_VMEM if single else [IN_VMEM] * len(out_shape),
        scratch_shapes=list(scratch),
        compiler_params=pltpu.CompilerParams(vmem_limit_bytes=grant * MIB),
        cost_estimate=pl.CostEstimate(flops=flops, bytes_accessed=moved, transcendentals=0),
    )(*operands)


TILE = 384


def terms_of(at_ref, backs, weights, blocks, cols):
    total = None
    for i, (weight, block) in enumerate(zip(weights, blocks, strict=True)):
        acts = block[...]
        if backs[i // 2] == 3:
            acts = jnp.where(at_ref[1] == 3, acts, jnp.zeros_like(acts))
        term = jnp.dot(acts, weight[:, cols], preferred_element_type=F32)
        total = term if total is None else total + term
    return total


def split_blocks(refs):
    out = []
    for ref in refs:
        out += [ref.at[0], ref.at[1]] if len(ref.shape) == 3 else [ref]
    return out


def partial_kernel(backs, at_ref, *refs):
    weights, blocks, total_ref = refs[: 2 * len(backs)], refs[2 * len(backs) : -1], refs[-1]
    base_ref = None
    if len(blocks[0].shape) == 2 and blocks[0].shape == total_ref.shape:
        base_ref, *blocks = blocks
    blocks = split_blocks(blocks)
    for n in range(total_ref.shape[1] // TILE):
        cols = slice(n * TILE, (n + 1) * TILE)
        total = terms_of(at_ref, backs, weights, blocks, cols)
        total_ref[:, cols] = total if base_ref is None else total + base_ref[:, cols]


def partial(at, backs, blocks, weights, base=None):
    rows, cols = blocks[0].shape[-2], weights[0][0].shape[1]
    operands = [at] + [w for back in backs for w in weights[back]] + ([] if base is None else [base]) + blocks
    return call(
        functools.partial(partial_kernel, backs),
        jax.ShapeDtypeStruct((rows, cols), F32),
        operands, 12, flops=4 * len(backs) * rows * 512 * cols,
    )


def last_kernel(backs, at_ref, *refs):
    weights, (base_ref, *refs) = refs[: 2 * len(backs)], refs[2 * len(backs) :]
    turned = refs[-1]
    self_ref, *away = refs[-5:-1]
    blocks = split_blocks(refs[:-5])
    for n in range(base_ref.shape[1] // TILE):
        cols = slice(n * TILE, (n + 1) * TILE)
        total = terms_of(at_ref, backs, weights, blocks, cols) + base_ref[:, cols]
        turned[cols, :] = total.T
    for by in range(NX):
        owner = lax.rem(at_ref[2] + by, NX)
        for z in range(NZ):
            piece = turned[pl.ds(pl.multiple_of((z * NX + owner) * 72, 8), 72), :]
            if by == 0:
                self_ref[z] = piece
            else:
                away[by - 1][z] = piece.astype(BF)


def last(at, base, backs, blocks, weights):
    rows, cols = base.shape
    piece = (NZ, cols // (NX * NZ), rows)
    return call(
        functools.partial(last_kernel, backs),
        [jax.ShapeDtypeStruct(piece, F32)] + [jax.ShapeDtypeStruct(piece, BF)] * 3,
        [at] + [w for back in backs for w in weights[back]] + [base] + blocks, 12,
        scratch=[pltpu.VMEM((cols, rows), F32)], flops=4 * rows * 512 * cols,
    )


def x_sum_kernel(at_ref, *refs):
    *before, self_ref, a_ref, b_ref, c_ref, out_ref = refs
    for z in range(NZ):
        total = self_ref[z] + a_ref[z].astype(F32) + b_ref[z].astype(F32) + c_ref[z].astype(F32)
        total = total.astype(BF)
        for c, piece in enumerate((total[:36], total[36:])):
            if before:
                out_ref[2 * z + c, :36] = before[0][2 * z + c]
                out_ref[2 * z + c, 36:] = piece
            else:
                out_ref[2 * z + c] = piece


def x_sum(at, before, kept, came):
    shape = (2 * NZ, 72 if before else 36, 256)
    return call(x_sum_kernel, jax.ShapeDtypeStruct(shape, BF), [at, *before, kept, *came], 8)


def final_kernel(at_ref, chips_ref, bias_ref, out_ref):
    for c in range(2):
        chips = chips_ref[c].astype(F32)
        for z in range(1, NZ):
            chips = chips + chips_ref[2 * z + c].astype(F32)
        for block in range(2):
            total = (chips[block * 36 : (block + 1) * 36] + bias_ref[...]).astype(BF)
            for dp in range(2):

                @pl.when(at_ref[3] == dp)
                def _(total=total, start=(dp ^ block) * 512 + c * 256):
                    out_ref[:, start : start + 256] = total


def finish(at, chips, bias):
    return call(final_kernel, jax.ShapeDtypeStruct((36, 1024), BF), [at, chips, bias], 8)


def per_device(resid, enc_weight, enc_bias, dec_weight, dec_bias, lengths):
    target, feat, dp = lax.axis_index("layer"), lax.axis_index("feat"), lax.axis_index("dp")
    core = feat % 2
    at = jnp.stack([core, target, feat // 2 % NX, dp]).astype(jnp.int32)
    valid = (jnp.arange(SEQ)[None, :] < lengths[:, None]).reshape(-1).astype(F32)
    pre = jnp.dot(resid[0], enc_weight[0], preferred_element_type=F32) + enc_bias
    acts = (jax.nn.relu(pre) * valid[:, None]).astype(BF).reshape(2, 256, 512)
    keep = lax.dynamic_index_in_dim(acts, core, 0, keepdims=False)
    send = lax.dynamic_index_in_dim(acts, 1 - core, 0, keepdims=False)
    across = lambda flip: [(d * 32 + f, (1 - d) * 32 + (f ^ flip)) for d in range(2) for f in range(32)]
    other_mine = lax.ppermute(keep, ("dp", "feat"), across(0))
    other_theirs = lax.ppermute(send, ("dp", "feat"), across(1))
    own_theirs = lax.ppermute(send, "feat", PARTNER)
    w_theirs = lax.ppermute(dec_weight, "feat", PARTNER)
    weights = [
        [lax.dynamic_index_in_dim(w[0], jnp.maximum(target - back, 0), 0, keepdims=False) for w in (dec_weight, w_theirs)]
        for back in range(4)
    ]
    chips = []
    for mine, theirs in ((keep, own_theirs), (other_mine, other_theirs)):
        both = jnp.stack([mine, theirs])
        up = lax.ppermute(both, "layer", [(0, 1), (1, 2), (2, 3)])
        down = lax.ppermute(both, "layer", [(0, 3), (1, 0)])
        far_up = lax.ppermute(up[0], "layer", [(1, 2), (2, 3)])
        far_down = lax.ppermute(down[1], "layer", [(3, 2), (0, 3)])
        total = partial(at, (0,), [both], weights)
        total = partial(at, (1, 3), [up, down], weights, total)
        kept, *away = last(at, total, (2,), [far_up, far_down], weights)
        came = []
        for by, piece in enumerate(away):
            came.append(lax.ppermute(piece, "feat", x_pairs(by + 1)))
        chips = [x_sum(at, chips, kept, came)]
    chips = lax.all_to_all(chips[0], "feat", 0, 0, tiled=True, axis_index_groups=ZC_GROUPS)
    out = finish(at, chips, dec_bias.reshape(36, 1))
    return out.T[None]


def solution(mesh):
    in_specs = (
        P("layer", "dp", None),
        P("layer", None, "feat"),
        P("layer", "feat"),
        P("layer", None, "feat", "dp"),
        P("layer", ("dp", "feat")),
        P("dp"),
    )
    out_specs = P("layer", None, ("dp", "feat"))


    return jax.shard_map(per_device, mesh=mesh, in_specs=in_specs, out_specs=out_specs, check_vma=False)
```

```python
import functools

import jax
import jax.numpy as jnp
from jax import lax
from jax.experimental import pallas as pl
from jax.experimental.pallas import tpu as pltpu
from jax.sharding import PartitionSpec as P


SEQ = 128
BF = jnp.bfloat16
F32 = jnp.float32

NX, NZ = 4, 4
PARTNER = [(i, i ^ 1) for i in range(32)]


def feat_at(z, x, c):
    return z * 8 + x * 2 + c


def x_pairs(by):
    return [
        (feat_at(z, x, c), feat_at(z, (x + by) % NX, c))
        for z in range(NZ) for x in range(NX) for c in range(2)
    ]


ZC_GROUPS = [[feat_at(z, x, c) for z in range(NZ) for c in range(2)] for x in range(NX)]


IN_VMEM = pl.BlockSpec(memory_space=pltpu.VMEM)
IN_SMEM = pl.BlockSpec(memory_space=pltpu.SMEM)
MIB = 1 << 20


def call(kernel, out_shape, operands, grant, scratch=(), flops=0):
    single = not isinstance(out_shape, (list, tuple))
    moved = sum(a.size * a.dtype.itemsize for a in operands)
    return pl.pallas_call(
        kernel,
        out_shape=out_shape,
        in_specs=[IN_SMEM] + [IN_VMEM] * (len(operands) - 1),
        out_specs=IN_VMEM if single else [IN_VMEM] * len(out_shape),
        scratch_shapes=list(scratch),
        compiler_params=pltpu.CompilerParams(vmem_limit_bytes=grant * MIB),
        cost_estimate=pl.CostEstimate(flops=flops, bytes_accessed=moved, transcendentals=0),
    )(*operands)


TILE = 384
GRANT = 12


def terms_of(at_ref, backs, weights, blocks, cols):
    total = None
    for i, block in enumerate(blocks):
        back = backs[i // 2]
        acts = block[...]
        if back == 3:
            acts = jnp.where(at_ref[1] == 3, acts, jnp.zeros_like(acts))
        term = jnp.dot(acts, weights[i][:, cols], preferred_element_type=F32)
        total = term if total is None else total + term
    return total


def split_blocks(refs):
    out = []
    for ref in refs:
        out += [ref.at[0], ref.at[1]] if len(ref.shape) == 3 else [ref]
    return out


def pick(weights, backs):
    return [w for back in backs for w in weights[back]]


def partial_kernel(backs, at_ref, *refs):
    weights, blocks, total_ref = refs[: 2 * len(backs)], refs[2 * len(backs) : -1], refs[-1]
    blocks = split_blocks(blocks)
    for n in range(total_ref.shape[1] // TILE):
        cols = slice(n * TILE, (n + 1) * TILE)
        total_ref[:, cols] = terms_of(at_ref, backs, weights, blocks, cols)


def partial(at, weights, backs, blocks):
    rows, cols = blocks[0].shape[-2], weights[0][0].shape[1]
    return call(
        functools.partial(partial_kernel, backs),
        jax.ShapeDtypeStruct((rows, cols), F32),
        [at, *pick(weights, backs), *blocks], GRANT, flops=4 * len(backs) * rows * 512 * cols,
    )


def last_kernel(backs, has_base, at_ref, *refs):
    weights, refs = refs[: 2 * len(backs)], refs[2 * len(backs) :]
    turned = refs[-1]
    self_ref, *away = refs[-5:-1]
    refs = refs[:-5]
    blocks = split_blocks(refs[has_base:])
    for n in range(turned.shape[0] // TILE):
        cols = slice(n * TILE, (n + 1) * TILE)
        total = terms_of(at_ref, backs, weights, blocks, cols)
        if has_base:
            total = total + refs[0][:, cols]
        turned[cols, :] = total.T
    for by in range(NX):
        owner = lax.rem(at_ref[2] + by, NX)
        for z in range(NZ):
            piece = turned[pl.ds(pl.multiple_of((z * NX + owner) * 72, 8), 72), :]
            if by == 0:
                self_ref[z] = piece
            else:
                away[by - 1][z] = piece.astype(BF)


def last(at, weights, base, backs, blocks):
    rows, cols = blocks[0].shape[-2], weights[0][0].shape[1]
    piece = (NZ, cols // (NX * NZ), rows)
    return call(
        functools.partial(last_kernel, backs, len(base)),
        [jax.ShapeDtypeStruct(piece, F32)] + [jax.ShapeDtypeStruct(piece, BF)] * 3,
        [at, *pick(weights, backs), *base, *blocks], GRANT,
        scratch=[pltpu.VMEM((cols, rows), F32)], flops=4 * len(backs) * rows * 512 * cols,
    )


def x_sum_kernel(at_ref, *refs):
    *before, self_ref, a_ref, b_ref, c_ref, out_ref = refs
    for z in range(NZ):
        total = self_ref[z] + a_ref[z].astype(F32) + b_ref[z].astype(F32) + c_ref[z].astype(F32)
        total = total.astype(BF)
        for c, piece in enumerate((total[:36], total[36:])):
            if before:
                out_ref[2 * z + c, :36] = before[0][2 * z + c]
                out_ref[2 * z + c, 36:] = piece
            else:
                out_ref[2 * z + c] = piece


def x_sum(at, before, kept, came):
    shape = (2 * NZ, 72 if before else 36, 256)
    return call(x_sum_kernel, jax.ShapeDtypeStruct(shape, BF), [at, *before, kept, *came], 8)


def final_kernel(at_ref, chips_ref, bias_ref, out_ref):
    for c in range(2):
        chips = chips_ref[c].astype(F32)
        for z in range(1, NZ):
            chips = chips + chips_ref[2 * z + c].astype(F32)
        for block in range(2):
            total = (chips[block * 36 : (block + 1) * 36] + bias_ref[...]).astype(BF)
            for dp in range(2):

                @pl.when(at_ref[3] == dp)
                def _(total=total, start=(dp ^ block) * 512 + c * 256):
                    out_ref[:, start : start + 256] = total


def finish(at, chips, bias):
    return call(final_kernel, jax.ShapeDtypeStruct((36, 1024), BF), [at, chips, bias], 8)


def per_device(resid, enc_weight, enc_bias, dec_weight, dec_bias, lengths):
    target, feat, dp = lax.axis_index("layer"), lax.axis_index("feat"), lax.axis_index("dp")
    core = feat % 2
    at = jnp.stack([core, target, feat // 2 % NX, dp]).astype(jnp.int32)
    w_theirs = lax.ppermute(dec_weight, "feat", PARTNER)
    valid = (jnp.arange(SEQ)[None, :] < lengths[:, None]).reshape(-1).astype(F32)
    pre = jnp.dot(resid[0], enc_weight[0], preferred_element_type=F32) + enc_bias
    acts = (jax.nn.relu(pre) * valid[:, None]).astype(BF).reshape(2, 256, 512)
    keep = lax.dynamic_index_in_dim(acts, core, 0, keepdims=False)
    send = lax.dynamic_index_in_dim(acts, 1 - core, 0, keepdims=False)
    across = lambda flip: [(d * 32 + f, (1 - d) * 32 + (f ^ flip)) for d in range(2) for f in range(32)]
    other_mine = lax.ppermute(keep, ("dp", "feat"), across(0))
    other_theirs = lax.ppermute(send, ("dp", "feat"), across(1))
    own_theirs = lax.ppermute(send, "feat", PARTNER)
    sources = [jnp.maximum(target - back, 0) for back in range(4)]
    mine_w = [lax.dynamic_index_in_dim(dec_weight[0], s, 0, keepdims=False) for s in sources]
    theirs_w = [lax.dynamic_index_in_dim(w_theirs[0], s, 0, keepdims=False) for s in sources]
    weights = list(zip(mine_w, theirs_w))
    chips = []
    for name, mine, theirs in (("own", keep, own_theirs), ("other", other_mine, other_theirs)):
        both = jnp.stack([mine, theirs])
        up = lax.ppermute(both, "layer", [(0, 1), (1, 2), (2, 3)])
        down = lax.ppermute(both, "layer", [(0, 3), (1, 0)])
        far_up = lax.ppermute(up[0], "layer", [(1, 2), (2, 3)])
        far_down = lax.ppermute(down[1], "layer", [(3, 2), (0, 3)])
        near, far = [both, up, down], [far_up, far_down]
        if name == "own":
            kept, *away = last(at, weights, [], (0, 1, 3, 2), near + far)
        else:
            total = partial(at, weights, (0, 1, 3), near)
            kept, *away = last(at, weights, [total], (2,), far)
        came = []
        for by, piece in enumerate(away):
            came.append(lax.ppermute(piece, "feat", x_pairs(by + 1)))
        chips = [x_sum(at, chips, kept, came)]
    chips = lax.all_to_all(chips[0], "feat", 0, 0, tiled=True, axis_index_groups=ZC_GROUPS)
    out = finish(at, chips, dec_bias.reshape(36, 1))
    return out.T[None]


def solution(mesh):
    in_specs = (
        P("layer", "dp", None),
        P("layer", None, "feat"),
        P("layer", "feat"),
        P("layer", None, "feat", "dp"),
        P("layer", ("dp", "feat")),
        P("dp"),
    )
    out_specs = P("layer", None, ("dp", "feat"))


    return jax.shard_map(
        per_device, mesh=mesh, in_specs=in_specs, out_specs=out_specs, check_vma=False
    )
```

```python
import functools

import jax
import jax.numpy as jnp
from jax import lax
from jax.experimental import pallas as pl
from jax.experimental.pallas import tpu as pltpu
from jax.sharding import PartitionSpec as P


SEQ = 128
BF = jnp.bfloat16
F32 = jnp.float32

NX, NZ = 4, 4
PARTNER = [(i, i ^ 1) for i in range(32)]


def feat_at(z, x, c):
    return z * 8 + x * 2 + c


def x_pairs(by):
    return [
        (feat_at(z, x, c), feat_at(z, (x + by) % NX, c))
        for z in range(NZ) for x in range(NX) for c in range(2)
    ]


def ring(by):
    return [(i, (i + by) % 4) for i in range(4)]


ZC_GROUPS = [[feat_at(z, x, c) for z in range(NZ) for c in range(2)] for x in range(NX)]


IN_VMEM = pl.BlockSpec(memory_space=pltpu.VMEM)
IN_SMEM = pl.BlockSpec(memory_space=pltpu.SMEM)
MIB = 1 << 20


def call(kernel, out_shape, operands, grant, scratch=(), flops=0):
    single = not isinstance(out_shape, (list, tuple))
    moved = sum(a.size * a.dtype.itemsize for a in operands)
    return pl.pallas_call(
        kernel,
        out_shape=out_shape,
        in_specs=[IN_SMEM] + [IN_VMEM] * (len(operands) - 1),
        out_specs=IN_VMEM if single else [IN_VMEM] * len(out_shape),
        scratch_shapes=list(scratch),
        compiler_params=pltpu.CompilerParams(vmem_limit_bytes=grant * MIB),
        cost_estimate=pl.CostEstimate(flops=flops, bytes_accessed=moved, transcendentals=0),
    )(*operands)


TILE = 384
GRANT = 12


def terms_of(weights, blocks, cols):
    total = None
    for i, block in enumerate(blocks):
        term = jnp.dot(block[...], weights[i][:, cols], preferred_element_type=F32)
        total = term if total is None else total + term
    return total


def split_blocks(refs):
    out = []
    for ref in refs:
        out += [ref.at[0], ref.at[1]] if len(ref.shape) == 3 else [ref]
    return out


def pick(weights, backs):
    return [w for back in backs for w in weights[back]]


def partial_kernel(backs, at_ref, *refs):
    weights, blocks, total_ref = refs[: 2 * len(backs)], refs[2 * len(backs) : -1], refs[-1]
    blocks = split_blocks(blocks)
    for n in range(total_ref.shape[1] // TILE):
        cols = slice(n * TILE, (n + 1) * TILE)
        total_ref[:, cols] = terms_of(weights, blocks, cols)


def partial(at, weights, backs, blocks):
    rows, cols = blocks[0].shape[-2], weights[0][0].shape[1]
    return call(
        functools.partial(partial_kernel, backs),
        jax.ShapeDtypeStruct((rows, cols), F32),
        [at, *pick(weights, backs), *blocks], GRANT, flops=4 * len(backs) * rows * 512 * cols,
    )


def last_kernel(backs, has_base, at_ref, *refs):
    weights, refs = refs[: 2 * len(backs)], refs[2 * len(backs) :]
    turned = refs[-1]
    self_ref, *away = refs[-5:-1]
    refs = refs[:-5]
    blocks = split_blocks(refs[has_base:])
    for n in range(turned.shape[0] // TILE):
        cols = slice(n * TILE, (n + 1) * TILE)
        total = terms_of(weights, blocks, cols)
        if has_base:
            total = total + refs[0][:, cols]
        turned[cols, :] = total.T
    for by in range(NX):
        owner = lax.rem(at_ref[2] + by, NX)
        for z in range(NZ):
            piece = turned[pl.ds(pl.multiple_of((z * NX + owner) * 72, 8), 72), :]
            if by == 0:
                self_ref[z] = piece
            else:
                away[by - 1][z] = piece.astype(BF)


def last(at, weights, base, backs, blocks):
    rows, cols = blocks[0].shape[-2], weights[0][0].shape[1]
    piece = (NZ, cols // (NX * NZ), rows)
    return call(
        functools.partial(last_kernel, backs, len(base)),
        [jax.ShapeDtypeStruct(piece, F32)] + [jax.ShapeDtypeStruct(piece, BF)] * 3,
        [at, *pick(weights, backs), *base, *blocks], GRANT,
        scratch=[pltpu.VMEM((cols, rows), F32)], flops=4 * len(backs) * rows * 512 * cols,
    )


def x_sum_kernel(at_ref, *refs):
    *before, self_ref, a_ref, b_ref, c_ref, out_ref = refs
    for z in range(NZ):
        total = self_ref[z] + a_ref[z].astype(F32) + b_ref[z].astype(F32) + c_ref[z].astype(F32)
        total = total.astype(BF)
        for c, piece in enumerate((total[:36], total[36:])):
            if before:
                out_ref[2 * z + c, :36] = before[0][2 * z + c]
                out_ref[2 * z + c, 36:] = piece
            else:
                out_ref[2 * z + c] = piece


def x_sum(at, before, kept, came):
    shape = (2 * NZ, 72 if before else 36, 256)
    return call(x_sum_kernel, jax.ShapeDtypeStruct(shape, BF), [at, *before, kept, *came], 8)


def final_kernel(at_ref, chips_ref, bias_ref, out_ref):
    for c in range(2):
        chips = chips_ref[c].astype(F32)
        for z in range(1, NZ):
            chips = chips + chips_ref[2 * z + c].astype(F32)
        for block in range(2):
            total = (chips[block * 36 : (block + 1) * 36] + bias_ref[...]).astype(BF)
            for dp in range(2):

                @pl.when(at_ref[3] == dp)
                def _(total=total, start=(dp ^ block) * 512 + c * 256):
                    out_ref[:, start : start + 256] = total


def finish(at, chips, bias):
    return call(final_kernel, jax.ShapeDtypeStruct((36, 1024), BF), [at, chips, bias], 8)


def per_device(resid, enc_weight, enc_bias, dec_weight, dec_bias, lengths):
    target, feat, dp = lax.axis_index("layer"), lax.axis_index("feat"), lax.axis_index("dp")
    core = feat % 2
    at = jnp.stack([core, target, feat // 2 % NX, dp]).astype(jnp.int32)
    w_theirs = lax.ppermute(dec_weight, "feat", PARTNER)
    valid = (jnp.arange(SEQ)[None, :] < lengths[:, None]).reshape(-1).astype(F32)
    pre = jnp.dot(resid[0], enc_weight[0], preferred_element_type=F32) + enc_bias
    acts = (jax.nn.relu(pre) * valid[:, None]).astype(BF).reshape(2, 256, 512)
    keep = lax.dynamic_index_in_dim(acts, core, 0, keepdims=False)
    send = lax.dynamic_index_in_dim(acts, 1 - core, 0, keepdims=False)
    across = lambda flip: [(d * 32 + f, (1 - d) * 32 + (f ^ flip)) for d in range(2) for f in range(32)]
    other_mine = lax.ppermute(keep, ("dp", "feat"), across(0))
    other_theirs = lax.ppermute(send, ("dp", "feat"), across(1))
    own_theirs = lax.ppermute(send, "feat", PARTNER)
    def cut(decoders, back):
        matrix = lax.dynamic_index_in_dim(decoders[0], jnp.maximum(target - back, 0), 0, keepdims=False)
        return jnp.where(target >= back, matrix, jnp.zeros_like(matrix)) if back else matrix

    mine_w = [cut(dec_weight, back) for back in range(4)]
    theirs_w = [cut(w_theirs, back) for back in range(4)]
    weights = list(zip(mine_w, theirs_w))
    chips = []
    for name, mine, theirs in (("own", keep, own_theirs), ("other", other_mine, other_theirs)):
        both = jnp.stack([mine, theirs])
        up = lax.ppermute(both, "layer", ring(1))
        down = lax.ppermute(both, "layer", ring(-1))
        far_up = lax.ppermute(up[0], "layer", ring(1))
        far_down = lax.ppermute(down[1], "layer", ring(-1))
        near, far = [both, up, down], [far_up, far_down]
        if name == "own":
            kept, *away = last(at, weights, [], (0, 1, 3, 2), near + far)
        else:
            total = partial(at, weights, (0, 1, 3), near)
            kept, *away = last(at, weights, [total], (2,), far)
        came = []
        for by, piece in enumerate(away):
            came.append(lax.ppermute(piece, "feat", x_pairs(by + 1)))
        chips = [x_sum(at, chips, kept, came)]
    chips = lax.all_to_all(chips[0], "feat", 0, 0, tiled=True, axis_index_groups=ZC_GROUPS)
    out = finish(at, chips, dec_bias.reshape(36, 1))
    return out.T[None]


def solution(mesh):
    in_specs = (
        P("layer", "dp", None),
        P("layer", None, "feat"),
        P("layer", "feat"),
        P("layer", None, "feat", "dp"),
        P("layer", ("dp", "feat")),
        P("dp"),
    )
    out_specs = P("layer", None, ("dp", "feat"))


    return jax.shard_map(per_device, mesh=mesh, in_specs=in_specs, out_specs=out_specs, check_vma=False)
```

```python
import functools

import jax
import jax.numpy as jnp
from jax import lax
from jax.experimental import pallas as pl
from jax.experimental.pallas import tpu as pltpu
from jax.sharding import PartitionSpec as P


SEQ = 128
BF = jnp.bfloat16
F32 = jnp.float32

NX, NZ = 4, 4
PARTNER = [(i, i ^ 1) for i in range(32)]


def feat_at(z, x, c):
    return z * 8 + x * 2 + c


def x_pairs(by):
    return [
        (feat_at(z, x, c), feat_at(z, (x + by) % NX, c))
        for z in range(NZ) for x in range(NX) for c in range(2)
    ]


def ring(by):
    return [(i, (i + by) % 4) for i in range(4)]


ZC_GROUPS = [[feat_at(z, x, c) for z in range(NZ) for c in range(2)] for x in range(NX)]


IN_VMEM = pl.BlockSpec(memory_space=pltpu.VMEM)
IN_SMEM = pl.BlockSpec(memory_space=pltpu.SMEM)
MIB = 1 << 20


def call(kernel, out_shape, operands, grant, scratch=(), flops=0):
    single = not isinstance(out_shape, (list, tuple))
    moved = sum(a.size * a.dtype.itemsize for a in operands)
    return pl.pallas_call(
        kernel,
        out_shape=out_shape,
        in_specs=[IN_SMEM] + [IN_VMEM] * (len(operands) - 1),
        out_specs=IN_VMEM if single else [IN_VMEM] * len(out_shape),
        scratch_shapes=list(scratch),
        compiler_params=pltpu.CompilerParams(vmem_limit_bytes=grant * MIB),
        cost_estimate=pl.CostEstimate(flops=flops, bytes_accessed=moved, transcendentals=0),
    )(*operands)


TILE = 384
GRANT = 12


def terms_of(backs, weights, blocks, cols):
    total = None
    for i, block in enumerate(blocks):
        term = jnp.dot(block[...], weights[i % 2][backs[i // 2], :, cols], preferred_element_type=F32)
        total = term if total is None else total + term
    return total


def split_blocks(refs):
    out = []
    for ref in refs:
        out += [ref.at[0], ref.at[1]] if len(ref.shape) == 3 else [ref]
    return out


def cut_kernel(at_ref, decoders_ref, out_ref, sems):
    target = at_ref[1]
    copies = [
        pltpu.make_async_copy(decoders_ref.at[0, jnp.maximum(target - back, 0)], out_ref.at[back], sems.at[back])
        for back in range(4)
    ]
    for copy in copies:
        copy.start()
    for back, copy in enumerate(copies):
        copy.wait()
        if back:

            @pl.when(target < back)
            def _(back=back):
                out_ref[back] = jnp.zeros_like(out_ref[back])


def cut(at, decoders):
    return pl.pallas_call(
        cut_kernel,
        out_shape=jax.ShapeDtypeStruct(decoders.shape[1:], BF),
        in_specs=[IN_SMEM, pl.BlockSpec(memory_space=pltpu.HBM)],
        out_specs=IN_VMEM,
        scratch_shapes=[pltpu.SemaphoreType.DMA((4,))],
        compiler_params=pltpu.CompilerParams(vmem_limit_bytes=6 * MIB),
        cost_estimate=pl.CostEstimate(flops=0, bytes_accessed=2 * decoders.size, transcendentals=0),
        name="cut",
    )(at, decoders)


def partial_kernel(backs, at_ref, *refs):
    weights, blocks, total_ref = refs[:2], refs[2:-1], refs[-1]
    blocks = split_blocks(blocks)
    for n in range(total_ref.shape[1] // TILE):
        cols = slice(n * TILE, (n + 1) * TILE)
        total_ref[:, cols] = terms_of(backs, weights, blocks, cols)


def partial(at, weights, backs, blocks):
    rows, cols = blocks[0].shape[-2], weights[0].shape[2]
    return call(
        functools.partial(partial_kernel, backs),
        jax.ShapeDtypeStruct((rows, cols), F32),
        [at, *weights, *blocks], GRANT, flops=4 * len(backs) * rows * 512 * cols,
    )


def last_kernel(backs, has_base, at_ref, *refs):
    weights, refs = refs[:2], refs[2:]
    turned = refs[-1]
    self_ref, *away = refs[-5:-1]
    refs = refs[:-5]
    blocks = split_blocks(refs[has_base:])
    for n in range(turned.shape[0] // TILE):
        cols = slice(n * TILE, (n + 1) * TILE)
        total = terms_of(backs, weights, blocks, cols)
        if has_base:
            total = total + refs[0][:, cols]
        turned[cols, :] = total.T
    for by in range(NX):
        owner = lax.rem(at_ref[2] + by, NX)
        for z in range(NZ):
            piece = turned[pl.ds(pl.multiple_of((z * NX + owner) * 72, 8), 72), :]
            if by == 0:
                self_ref[z] = piece
            else:
                away[by - 1][z] = piece.astype(BF)


def last(at, weights, base, backs, blocks):
    rows, cols = blocks[0].shape[-2], weights[0].shape[2]
    piece = (NZ, cols // (NX * NZ), rows)
    return call(
        functools.partial(last_kernel, backs, len(base)),
        [jax.ShapeDtypeStruct(piece, F32)] + [jax.ShapeDtypeStruct(piece, BF)] * 3,
        [at, *weights, *base, *blocks], GRANT,
        scratch=[pltpu.VMEM((cols, rows), F32)], flops=4 * len(backs) * rows * 512 * cols,
    )


def x_sum_kernel(at_ref, *refs):
    *before, self_ref, a_ref, b_ref, c_ref, out_ref = refs
    for z in range(NZ):
        total = self_ref[z] + a_ref[z].astype(F32) + b_ref[z].astype(F32) + c_ref[z].astype(F32)
        total = total.astype(BF)
        for c, piece in enumerate((total[:36], total[36:])):
            if before:
                out_ref[2 * z + c, :36] = before[0][2 * z + c]
                out_ref[2 * z + c, 36:] = piece
            else:
                out_ref[2 * z + c] = piece


def x_sum(at, before, kept, came):
    shape = (2 * NZ, 72 if before else 36, 256)
    return call(x_sum_kernel, jax.ShapeDtypeStruct(shape, BF), [at, *before, kept, *came], 8)


def final_kernel(at_ref, chips_ref, bias_ref, out_ref):
    for c in range(2):
        chips = chips_ref[c].astype(F32)
        for z in range(1, NZ):
            chips = chips + chips_ref[2 * z + c].astype(F32)
        for block in range(2):
            total = (chips[block * 36 : (block + 1) * 36] + bias_ref[...]).astype(BF)
            for dp in range(2):

                @pl.when(at_ref[3] == dp)
                def _(total=total, start=(dp ^ block) * 512 + c * 256):
                    out_ref[:, start : start + 256] = total


def finish(at, chips, bias):
    return call(final_kernel, jax.ShapeDtypeStruct((36, 1024), BF), [at, chips, bias], 8)


def per_device(resid, enc_weight, enc_bias, dec_weight, dec_bias, lengths):
    target, feat, dp = lax.axis_index("layer"), lax.axis_index("feat"), lax.axis_index("dp")
    core = feat % 2
    at = jnp.stack([core, target, feat // 2 % NX, dp]).astype(jnp.int32)
    w_theirs = lax.ppermute(dec_weight, "feat", PARTNER)
    valid = (jnp.arange(SEQ)[None, :] < lengths[:, None]).reshape(-1).astype(F32)
    pre = jnp.dot(resid[0], enc_weight[0], preferred_element_type=F32) + enc_bias
    acts = (jax.nn.relu(pre) * valid[:, None]).astype(BF).reshape(2, 256, 512)
    keep = lax.dynamic_index_in_dim(acts, core, 0, keepdims=False)
    send = lax.dynamic_index_in_dim(acts, 1 - core, 0, keepdims=False)
    across = lambda flip: [(d * 32 + f, (1 - d) * 32 + (f ^ flip)) for d in range(2) for f in range(32)]
    other_mine = lax.ppermute(keep, ("dp", "feat"), across(0))
    other_theirs = lax.ppermute(send, ("dp", "feat"), across(1))
    own_theirs = lax.ppermute(send, "feat", PARTNER)
    mine_w = cut(at, dec_weight)
    theirs_w = cut(at, w_theirs)
    weights = (mine_w, theirs_w)
    chips = []
    for mine, theirs in ((keep, own_theirs), (other_mine, other_theirs)):
        both = jnp.stack([mine, theirs])
        up = lax.ppermute(both, "layer", ring(1))
        down = lax.ppermute(both, "layer", ring(-1))
        far_up = lax.ppermute(up[0], "layer", ring(1))
        far_down = lax.ppermute(down[1], "layer", ring(-1))
        near, far = [both, up, down], [far_up, far_down]
        total = partial(at, weights, (0, 1, 3), near)
        kept, *away = last(at, weights, [total], (2,), far)
        came = []
        for by, piece in enumerate(away):
            came.append(lax.ppermute(piece, "feat", x_pairs(by + 1)))
        chips = [x_sum(at, chips, kept, came)]
    chips = lax.all_to_all(chips[0], "feat", 0, 0, tiled=True, axis_index_groups=ZC_GROUPS)
    out = finish(at, chips, dec_bias.reshape(36, 1))
    return out.T[None]


def solution(mesh):
    in_specs = (
        P("layer", "dp", None),
        P("layer", None, "feat"),
        P("layer", "feat"),
        P("layer", None, "feat", "dp"),
        P("layer", ("dp", "feat")),
        P("dp"),
    )
    out_specs = P("layer", None, ("dp", "feat"))


    return jax.shard_map(per_device, mesh=mesh, in_specs=in_specs, out_specs=out_specs, check_vma=False)
```

```python
import functools

import jax
import jax.numpy as jnp
from jax import lax
from jax.experimental import pallas as pl
from jax.experimental.pallas import tpu as pltpu
from jax.sharding import PartitionSpec as P


SEQ = 128
BF = jnp.bfloat16
F32 = jnp.float32

NX, NZ = 4, 4
PARTNER = [(i, i ^ 1) for i in range(32)]


def feat_at(z, x, c):
    return z * 8 + x * 2 + c


def x_pairs(by):
    return [
        (feat_at(z, x, c), feat_at(z, (x + by) % NX, c))
        for z in range(NZ) for x in range(NX) for c in range(2)
    ]


def ring(by):
    return [(i, (i + by) % 4) for i in range(4)]


ZC_GROUPS = [[feat_at(z, x, c) for z in range(NZ) for c in range(2)] for x in range(NX)]


IN_VMEM = pl.BlockSpec(memory_space=pltpu.VMEM)
IN_SMEM = pl.BlockSpec(memory_space=pltpu.SMEM)
MIB = 1 << 20


def call(kernel, out_shape, operands, grant, scratch=(), flops=0):
    single = not isinstance(out_shape, (list, tuple))
    moved = sum(a.size * a.dtype.itemsize for a in operands)
    return pl.pallas_call(
        kernel,
        out_shape=out_shape,
        in_specs=[IN_SMEM] + [IN_VMEM] * (len(operands) - 1),
        out_specs=IN_VMEM if single else [IN_VMEM] * len(out_shape),
        scratch_shapes=list(scratch),
        compiler_params=pltpu.CompilerParams(vmem_limit_bytes=grant * MIB),
        cost_estimate=pl.CostEstimate(flops=flops, bytes_accessed=moved, transcendentals=0),
    )(*operands)


TILE = 384
GRANT = 12
CUT_GRANT = 48


def terms_of(backs, weights, blocks, cols):
    total = None
    for i, block in enumerate(blocks):
        term = jnp.dot(block[...], weights[i % 2][backs[i // 2], :, cols], preferred_element_type=F32)
        total = term if total is None else total + term
    return total


def split_blocks(refs):
    out = []
    for ref in refs:
        out += [ref.at[0], ref.at[1]] if len(ref.shape) == 3 else [ref]
    return out


def cut_kernel(at_ref, mine_ref, theirs_ref, mine_out, theirs_out, sems):
    target = at_ref[1]
    copies = [
        pltpu.make_async_copy(src.at[0, jnp.maximum(target - back, 0)], out.at[back], sems.at[i, back])
        for i, (src, out) in enumerate(((mine_ref, mine_out), (theirs_ref, theirs_out)))
        for back in range(4)
    ]
    for copy in copies:
        copy.start()
    for copy in copies:
        copy.wait()
    for back in range(1, 4):

        @pl.when(target < back)
        def _(back=back):
            for out in (mine_out, theirs_out):
                out[back] = jnp.zeros_like(out[back])


def cut(at, mine, theirs):
    in_hbm = pl.BlockSpec(memory_space=pltpu.HBM)
    return pl.pallas_call(
        cut_kernel,
        out_shape=[jax.ShapeDtypeStruct(mine.shape[1:], BF)] * 2,
        in_specs=[IN_SMEM, in_hbm, in_hbm],
        out_specs=[IN_VMEM] * 2,
        scratch_shapes=[pltpu.SemaphoreType.DMA((2, 4))],
        compiler_params=pltpu.CompilerParams(vmem_limit_bytes=CUT_GRANT * MIB),
        cost_estimate=pl.CostEstimate(flops=0, bytes_accessed=4 * mine.size, transcendentals=0),
        name="cut",
    )(at, mine, theirs)


def partial_kernel(backs, at_ref, *refs):
    weights, blocks, total_ref = refs[:2], refs[2:-1], refs[-1]
    blocks = split_blocks(blocks)
    for n in range(total_ref.shape[1] // TILE):
        cols = slice(n * TILE, (n + 1) * TILE)
        total_ref[:, cols] = terms_of(backs, weights, blocks, cols)


def partial(at, weights, backs, blocks):
    rows, cols = blocks[0].shape[-2], weights[0].shape[2]
    return call(
        functools.partial(partial_kernel, backs),
        jax.ShapeDtypeStruct((rows, cols), F32),
        [at, *weights, *blocks], GRANT, flops=4 * len(backs) * rows * 512 * cols,
    )


def last_kernel(backs, has_base, at_ref, *refs):
    weights, refs = refs[:2], refs[2:]
    turned = refs[-1]
    self_ref, *away = refs[-5:-1]
    refs = refs[:-5]
    blocks = split_blocks(refs[has_base:])
    for n in range(turned.shape[0] // TILE):
        cols = slice(n * TILE, (n + 1) * TILE)
        total = terms_of(backs, weights, blocks, cols)
        if has_base:
            total = total + refs[0][:, cols]
        turned[cols, :] = total.T
    for by in range(NX):
        owner = lax.rem(at_ref[2] + by, NX)
        for z in range(NZ):
            piece = turned[pl.ds(pl.multiple_of((z * NX + owner) * 72, 8), 72), :]
            if by == 0:
                self_ref[z] = piece
            else:
                away[by - 1][z] = piece.astype(BF)


def last(at, weights, base, backs, blocks):
    rows, cols = blocks[0].shape[-2], weights[0].shape[2]
    piece = (NZ, cols // (NX * NZ), rows)
    return call(
        functools.partial(last_kernel, backs, len(base)),
        [jax.ShapeDtypeStruct(piece, F32)] + [jax.ShapeDtypeStruct(piece, BF)] * 3,
        [at, *weights, *base, *blocks], GRANT,
        scratch=[pltpu.VMEM((cols, rows), F32)], flops=4 * len(backs) * rows * 512 * cols,
    )


def x_sum_kernel(at_ref, *refs):
    *before, self_ref, a_ref, b_ref, c_ref, out_ref = refs
    for z in range(NZ):
        total = self_ref[z] + a_ref[z].astype(F32) + b_ref[z].astype(F32) + c_ref[z].astype(F32)
        total = total.astype(BF)
        for c, piece in enumerate((total[:36], total[36:])):
            if before:
                out_ref[2 * z + c, :36] = before[0][2 * z + c]
                out_ref[2 * z + c, 36:] = piece
            else:
                out_ref[2 * z + c] = piece


def x_sum(at, before, kept, came):
    shape = (2 * NZ, 72 if before else 36, 256)
    return call(x_sum_kernel, jax.ShapeDtypeStruct(shape, BF), [at, *before, kept, *came], 8)


def final_kernel(at_ref, chips_ref, bias_ref, out_ref):
    for c in range(2):
        chips = chips_ref[c].astype(F32)
        for z in range(1, NZ):
            chips = chips + chips_ref[2 * z + c].astype(F32)
        for block in range(2):
            total = (chips[block * 36 : (block + 1) * 36] + bias_ref[...]).astype(BF)
            for dp in range(2):

                @pl.when(at_ref[3] == dp)
                def _(total=total, start=(dp ^ block) * 512 + c * 256):
                    out_ref[:, start : start + 256] = total


def finish(at, chips, bias):
    return call(final_kernel, jax.ShapeDtypeStruct((36, 1024), BF), [at, chips, bias], 8)


def per_device(resid, enc_weight, enc_bias, dec_weight, dec_bias, lengths):
    target, feat, dp = lax.axis_index("layer"), lax.axis_index("feat"), lax.axis_index("dp")
    core = feat % 2
    at = jnp.stack([core, target, feat // 2 % NX, dp]).astype(jnp.int32)
    w_theirs = lax.ppermute(dec_weight, "feat", PARTNER)
    valid = (jnp.arange(SEQ)[None, :] < lengths[:, None]).reshape(-1).astype(F32)
    pre = jnp.dot(resid[0], enc_weight[0], preferred_element_type=F32) + enc_bias
    acts = (jax.nn.relu(pre) * valid[:, None]).astype(BF).reshape(2, 256, 512)
    keep = lax.dynamic_index_in_dim(acts, core, 0, keepdims=False)
    send = lax.dynamic_index_in_dim(acts, 1 - core, 0, keepdims=False)
    across = lambda flip: [(d * 32 + f, (1 - d) * 32 + (f ^ flip)) for d in range(2) for f in range(32)]
    other_mine = lax.ppermute(keep, ("dp", "feat"), across(0))
    other_theirs = lax.ppermute(send, ("dp", "feat"), across(1))
    own_theirs = lax.ppermute(send, "feat", PARTNER)
    weights = cut(at, dec_weight, w_theirs)
    chips = []
    for mine, theirs in ((keep, own_theirs), (other_mine, other_theirs)):
        both = jnp.stack([mine, theirs])
        up = lax.ppermute(both, "layer", ring(1))
        down = lax.ppermute(both, "layer", ring(-1))
        far_up = lax.ppermute(up[0], "layer", ring(1))
        far_down = lax.ppermute(down[1], "layer", ring(-1))
        near, far = [both, up, down], [far_up, far_down]
        total = partial(at, weights, (0, 1, 3), near)
        kept, *away = last(at, weights, [total], (2,), far)
        came = []
        for by, piece in enumerate(away):
            came.append(lax.ppermute(piece, "feat", x_pairs(by + 1)))
        chips = [x_sum(at, chips, kept, came)]
    chips = lax.all_to_all(chips[0], "feat", 0, 0, tiled=True, axis_index_groups=ZC_GROUPS)
    out = finish(at, chips, dec_bias.reshape(36, 1))
    return out.T[None]


def solution(mesh):
    in_specs = (
        P("layer", "dp", None),
        P("layer", None, "feat"),
        P("layer", "feat"),
        P("layer", None, "feat", "dp"),
        P("layer", ("dp", "feat")),
        P("dp"),
    )
    out_specs = P("layer", None, ("dp", "feat"))


    return jax.shard_map(per_device, mesh=mesh, in_specs=in_specs, out_specs=out_specs, check_vma=False)
```

```python
import functools

import jax
import jax.numpy as jnp
from jax import lax
from jax.experimental import pallas as pl
from jax.experimental.pallas import tpu as pltpu
from jax.sharding import PartitionSpec as P


SEQ = 128
BF = jnp.bfloat16
F32 = jnp.float32

NX, NZ = 4, 4
PARTNER = [(i, i ^ 1) for i in range(32)]


def feat_at(z, x, c):
    return z * 8 + x * 2 + c


def x_pairs(by):
    return [
        (feat_at(z, x, c), feat_at(z, (x + by) % NX, c))
        for z in range(NZ) for x in range(NX) for c in range(2)
    ]


def ring(by):
    return [(i, (i + by) % 4) for i in range(4)]


ZC_GROUPS = [[feat_at(z, x, c) for z in range(NZ) for c in range(2)] for x in range(NX)]


IN_VMEM = pl.BlockSpec(memory_space=pltpu.VMEM)
IN_SMEM = pl.BlockSpec(memory_space=pltpu.SMEM)
MIB = 1 << 20


def call(kernel, out_shape, operands, grant, scratch=(), flops=0):
    single = not isinstance(out_shape, (list, tuple))
    moved = sum(a.size * a.dtype.itemsize for a in operands)
    return pl.pallas_call(
        kernel,
        out_shape=out_shape,
        in_specs=[IN_SMEM] + [IN_VMEM] * (len(operands) - 1),
        out_specs=IN_VMEM if single else [IN_VMEM] * len(out_shape),
        scratch_shapes=list(scratch),
        compiler_params=pltpu.CompilerParams(vmem_limit_bytes=grant * MIB),
        cost_estimate=pl.CostEstimate(flops=flops, bytes_accessed=moved, transcendentals=0),
    )(*operands)


TILE = 384
GRANT = 12
CUT_GRANT = 6


def terms_of(backs, weights, blocks, cols):
    total = None
    for i, block in enumerate(blocks):
        term = jnp.dot(block[...], weights[i % 2][backs[i // 2], :, cols], preferred_element_type=F32)
        total = term if total is None else total + term
    return total


def split_blocks(refs):
    out = []
    for ref in refs:
        out += [ref.at[0], ref.at[1]] if len(ref.shape) == 3 else [ref]
    return out


def cut_kernel(at_ref, decoders_ref, out_ref, sems):
    target = at_ref[1]
    copies = [
        pltpu.make_async_copy(decoders_ref.at[0, jnp.maximum(target - back, 0)], out_ref.at[back], sems.at[back])
        for back in range(4)
    ]
    for copy in copies:
        copy.start()
    for back, copy in enumerate(copies):
        copy.wait()
        if back:

            @pl.when(target < back)
            def _(back=back):
                out_ref[back] = jnp.zeros_like(out_ref[back])


def cut(at, decoders):
    return pl.pallas_call(
        cut_kernel,
        out_shape=jax.ShapeDtypeStruct(decoders.shape[1:], BF),
        in_specs=[IN_SMEM, pl.BlockSpec(memory_space=pltpu.HBM)],
        out_specs=IN_VMEM,
        scratch_shapes=[pltpu.SemaphoreType.DMA((4,))],
        compiler_params=pltpu.CompilerParams(vmem_limit_bytes=CUT_GRANT * MIB),
        cost_estimate=pl.CostEstimate(flops=0, bytes_accessed=2 * decoders.size, transcendentals=0),
        name="cut",
    )(at, decoders)


def partial_kernel(backs, at_ref, *refs):
    weights, blocks, total_ref = refs[:2], refs[2:-1], refs[-1]
    blocks = split_blocks(blocks)
    for n in range(total_ref.shape[1] // TILE):
        cols = slice(n * TILE, (n + 1) * TILE)
        total_ref[:, cols] = terms_of(backs, weights, blocks, cols)


def partial(at, weights, backs, blocks):
    rows, cols = blocks[0].shape[-2], weights[0].shape[2]
    return call(
        functools.partial(partial_kernel, backs),
        jax.ShapeDtypeStruct((rows, cols), F32),
        [at, *weights, *blocks], GRANT, flops=4 * len(backs) * rows * 512 * cols,
    )


def last_kernel(backs, has_base, at_ref, *refs):
    weights, refs = refs[:2], refs[2:]
    turned = refs[-1]
    self_ref, *away = refs[-5:-1]
    refs = refs[:-5]
    blocks = split_blocks(refs[has_base:])
    for n in range(turned.shape[0] // TILE):
        cols = slice(n * TILE, (n + 1) * TILE)
        total = terms_of(backs, weights, blocks, cols)
        if has_base:
            total = total + refs[0][:, cols]
        turned[cols, :] = total.T
    for by in range(NX):
        owner = lax.rem(at_ref[2] + by, NX)
        for z in range(NZ):
            piece = turned[pl.ds(pl.multiple_of((z * NX + owner) * 72, 8), 72), :]
            if by == 0:
                self_ref[z] = piece
            else:
                away[by - 1][z] = piece.astype(BF)


def last(at, weights, base, backs, blocks):
    rows, cols = blocks[0].shape[-2], weights[0].shape[2]
    piece = (NZ, cols // (NX * NZ), rows)
    return call(
        functools.partial(last_kernel, backs, len(base)),
        [jax.ShapeDtypeStruct(piece, F32)] + [jax.ShapeDtypeStruct(piece, BF)] * 3,
        [at, *weights, *base, *blocks], GRANT,
        scratch=[pltpu.VMEM((cols, rows), F32)], flops=4 * len(backs) * rows * 512 * cols,
    )


def x_sum_kernel(at_ref, *refs):
    *before, self_ref, a_ref, b_ref, c_ref, out_ref = refs
    for z in range(NZ):
        total = self_ref[z] + a_ref[z].astype(F32) + b_ref[z].astype(F32) + c_ref[z].astype(F32)
        total = total.astype(BF)
        for c, piece in enumerate((total[:36], total[36:])):
            if before:
                out_ref[2 * z + c, :36] = before[0][2 * z + c]
                out_ref[2 * z + c, 36:] = piece
            else:
                out_ref[2 * z + c] = piece


def x_sum(at, before, kept, came):
    shape = (2 * NZ, 72 if before else 36, 256)
    return call(x_sum_kernel, jax.ShapeDtypeStruct(shape, BF), [at, *before, kept, *came], 8)


def final_kernel(at_ref, chips_ref, bias_ref, out_ref):
    for c in range(2):
        chips = chips_ref[c].astype(F32)
        for z in range(1, NZ):
            chips = chips + chips_ref[2 * z + c].astype(F32)
        for block in range(2):
            total = (chips[block * 36 : (block + 1) * 36] + bias_ref[...]).astype(BF)
            for dp in range(2):

                @pl.when(at_ref[3] == dp)
                def _(total=total, start=(dp ^ block) * 512 + c * 256):
                    out_ref[:, start : start + 256] = total


def finish(at, chips, bias):
    return call(final_kernel, jax.ShapeDtypeStruct((36, 1024), BF), [at, chips, bias], 8)


def per_device(resid, enc_weight, enc_bias, dec_weight, dec_bias, lengths):
    target, feat, dp = lax.axis_index("layer"), lax.axis_index("feat"), lax.axis_index("dp")
    core = feat % 2
    at = jnp.stack([core, target, feat // 2 % NX, dp]).astype(jnp.int32)
    valid = (jnp.arange(SEQ)[None, :] < lengths[:, None]).reshape(-1).astype(F32)
    pre = jnp.dot(resid[0], enc_weight[0], preferred_element_type=F32) + enc_bias
    acts = (jax.nn.relu(pre) * valid[:, None]).astype(BF).reshape(2, 256, 512)
    keep = lax.dynamic_index_in_dim(acts, core, 0, keepdims=False)
    send = lax.dynamic_index_in_dim(acts, 1 - core, 0, keepdims=False)
    across = lambda flip: [(d * 32 + f, (1 - d) * 32 + (f ^ flip)) for d in range(2) for f in range(32)]
    other_mine = lax.ppermute(keep, ("dp", "feat"), across(0))
    other_theirs = lax.ppermute(send, ("dp", "feat"), across(1))
    own_theirs = lax.ppermute(send, "feat", PARTNER)
    w_mine = cut(at, dec_weight)
    w_theirs = lax.ppermute(w_mine, "feat", PARTNER)
    weights = (w_mine, w_theirs)
    chips = []
    for mine, theirs in ((keep, own_theirs), (other_mine, other_theirs)):
        both = jnp.stack([mine, theirs])
        up = lax.ppermute(both, "layer", ring(1))
        down = lax.ppermute(both, "layer", ring(-1))
        far_up = lax.ppermute(up[0], "layer", ring(1))
        far_down = lax.ppermute(down[1], "layer", ring(-1))
        near, far = [both, up, down], [far_up, far_down]
        total = partial(at, weights, (0, 1, 3), near)
        kept, *away = last(at, weights, [total], (2,), far)
        came = []
        for by, piece in enumerate(away):
            came.append(lax.ppermute(piece, "feat", x_pairs(by + 1)))
        chips = [x_sum(at, chips, kept, came)]
    chips = lax.all_to_all(chips[0], "feat", 0, 0, tiled=True, axis_index_groups=ZC_GROUPS)
    out = finish(at, chips, dec_bias.reshape(36, 1))
    return out.T[None]


def solution(mesh):
    in_specs = (
        P("layer", "dp", None),
        P("layer", None, "feat"),
        P("layer", "feat"),
        P("layer", None, "feat", "dp"),
        P("layer", ("dp", "feat")),
        P("dp"),
    )
    out_specs = P("layer", None, ("dp", "feat"))


    return jax.shard_map(per_device, mesh=mesh, in_specs=in_specs, out_specs=out_specs, check_vma=False)
```

```python
import functools

import jax
import jax.numpy as jnp
from jax import lax
from jax.experimental import pallas as pl
from jax.experimental.pallas import tpu as pltpu
from jax.sharding import PartitionSpec as P


SEQ = 128
BF = jnp.bfloat16
F32 = jnp.float32

NX, NZ = 4, 4
PARTNER = [(i, i ^ 1) for i in range(32)]


def feat_at(z, x, c):
    return z * 8 + x * 2 + c


def x_pairs(by):
    return [
        (feat_at(z, x, c), feat_at(z, (x + by) % NX, c))
        for z in range(NZ) for x in range(NX) for c in range(2)
    ]


def ring(by):
    return [(i, (i + by) % 4) for i in range(4)]


ZC_GROUPS = [[feat_at(z, x, c) for z in range(NZ) for c in range(2)] for x in range(NX)]


IN_VMEM = pl.BlockSpec(memory_space=pltpu.VMEM)
IN_SMEM = pl.BlockSpec(memory_space=pltpu.SMEM)
MIB = 1 << 20


def call(kernel, out_shape, operands, grant, scratch=(), flops=0):
    single = not isinstance(out_shape, (list, tuple))
    moved = sum(a.size * a.dtype.itemsize for a in operands)
    return pl.pallas_call(
        kernel,
        out_shape=out_shape,
        in_specs=[IN_SMEM] + [IN_VMEM] * (len(operands) - 1),
        out_specs=IN_VMEM if single else [IN_VMEM] * len(out_shape),
        scratch_shapes=list(scratch),
        compiler_params=pltpu.CompilerParams(vmem_limit_bytes=grant * MIB),
        cost_estimate=pl.CostEstimate(flops=flops, bytes_accessed=moved, transcendentals=0),
    )(*operands)


TILE = 384
GRANT = 12
CUT_GRANT = 48


def terms_of(backs, weights, blocks, cols):
    total = None
    for i, block in enumerate(blocks):
        term = jnp.dot(block[...], weights[i % 2][backs[i // 2], :, cols], preferred_element_type=F32)
        total = term if total is None else total + term
    return total


def split_blocks(refs):
    out = []
    for ref in refs:
        out += [ref.at[0], ref.at[1]] if len(ref.shape) == 3 else [ref]
    return out


def cut_kernel(at_ref, decoders_ref, out_ref, sems):
    target = at_ref[1]
    copies = [
        pltpu.make_async_copy(decoders_ref.at[0, jnp.maximum(target - back, 0)], out_ref.at[back], sems.at[back])
        for back in range(4)
    ]
    for copy in copies:
        copy.start()
    for back, copy in enumerate(copies):
        copy.wait()
        if back:

            @pl.when(target < back)
            def _(back=back):
                out_ref[back] = jnp.zeros_like(out_ref[back])


def cut(at, decoders):
    return pl.pallas_call(
        cut_kernel,
        out_shape=jax.ShapeDtypeStruct(decoders.shape[1:], BF),
        in_specs=[IN_SMEM, pl.BlockSpec(memory_space=pltpu.HBM)],
        out_specs=IN_VMEM,
        scratch_shapes=[pltpu.SemaphoreType.DMA((4,))],
        compiler_params=pltpu.CompilerParams(vmem_limit_bytes=CUT_GRANT * MIB),
        cost_estimate=pl.CostEstimate(flops=0, bytes_accessed=2 * decoders.size, transcendentals=0),
        name="cut",
    )(at, decoders)


def partial_kernel(backs, at_ref, *refs):
    weights, blocks, total_ref = refs[:2], refs[2:-1], refs[-1]
    blocks = split_blocks(blocks)
    for n in range(total_ref.shape[1] // TILE):
        cols = slice(n * TILE, (n + 1) * TILE)
        total_ref[:, cols] = terms_of(backs, weights, blocks, cols)


def partial(at, weights, backs, blocks):
    rows, cols = blocks[0].shape[-2], weights[0].shape[2]
    return call(
        functools.partial(partial_kernel, backs),
        jax.ShapeDtypeStruct((rows, cols), F32),
        [at, *weights, *blocks], GRANT, flops=4 * len(backs) * rows * 512 * cols,
    )


def last_kernel(backs, has_base, at_ref, *refs):
    weights, refs = refs[:2], refs[2:]
    turned = refs[-1]
    self_ref, *away = refs[-5:-1]
    refs = refs[:-5]
    blocks = split_blocks(refs[has_base:])
    for n in range(turned.shape[0] // TILE):
        cols = slice(n * TILE, (n + 1) * TILE)
        total = terms_of(backs, weights, blocks, cols)
        if has_base:
            total = total + refs[0][:, cols]
        turned[cols, :] = total.T
    for by in range(NX):
        owner = lax.rem(at_ref[2] + by, NX)
        for z in range(NZ):
            piece = turned[pl.ds(pl.multiple_of((z * NX + owner) * 72, 8), 72), :]
            if by == 0:
                self_ref[z] = piece
            else:
                away[by - 1][z] = piece.astype(BF)


def last(at, weights, base, backs, blocks):
    rows, cols = blocks[0].shape[-2], weights[0].shape[2]
    piece = (NZ, cols // (NX * NZ), rows)
    return call(
        functools.partial(last_kernel, backs, len(base)),
        [jax.ShapeDtypeStruct(piece, F32)] + [jax.ShapeDtypeStruct(piece, BF)] * 3,
        [at, *weights, *base, *blocks], GRANT,
        scratch=[pltpu.VMEM((cols, rows), F32)], flops=4 * len(backs) * rows * 512 * cols,
    )


def decode(at, weights, near, far):
    total = partial(at, weights, (0, 1, 3), near)
    return last(at, weights, [total], (2,), far)


def x_sum_kernel(at_ref, *refs):
    *before, self_ref, a_ref, b_ref, c_ref, out_ref = refs
    for z in range(NZ):
        total = self_ref[z] + a_ref[z].astype(F32) + b_ref[z].astype(F32) + c_ref[z].astype(F32)
        total = total.astype(BF)
        for c, piece in enumerate((total[:36], total[36:])):
            if before:
                out_ref[2 * z + c, :36] = before[0][2 * z + c]
                out_ref[2 * z + c, 36:] = piece
            else:
                out_ref[2 * z + c] = piece


def x_sum(at, before, kept, came):
    shape = (2 * NZ, 72 if before else 36, 256)
    return call(x_sum_kernel, jax.ShapeDtypeStruct(shape, BF), [at, *before, kept, *came], 8)


def final_kernel(at_ref, chips_ref, bias_ref, out_ref):
    for c in range(2):
        chips = chips_ref[c].astype(F32)
        for z in range(1, NZ):
            chips = chips + chips_ref[2 * z + c].astype(F32)
        for block in range(2):
            total = (chips[block * 36 : (block + 1) * 36] + bias_ref[...]).astype(BF)
            for dp in range(2):

                @pl.when(at_ref[3] == dp)
                def _(total=total, start=(dp ^ block) * 512 + c * 256):
                    out_ref[:, start : start + 256] = total


def finish(at, chips, bias):
    return call(final_kernel, jax.ShapeDtypeStruct((36, 1024), BF), [at, chips, bias], 8)


def per_device(resid, enc_weight, enc_bias, dec_weight, dec_bias, lengths):
    target, feat, dp = lax.axis_index("layer"), lax.axis_index("feat"), lax.axis_index("dp")
    core = feat % 2
    at = jnp.stack([core, target, feat // 2 % NX, dp]).astype(jnp.int32)
    valid = (jnp.arange(SEQ)[None, :] < lengths[:, None]).reshape(-1).astype(F32)
    pre = jnp.dot(resid[0], enc_weight[0], preferred_element_type=F32) + enc_bias
    acts = (jax.nn.relu(pre) * valid[:, None]).astype(BF).reshape(2, 256, 512)
    keep = lax.dynamic_index_in_dim(acts, core, 0, keepdims=False)
    send = lax.dynamic_index_in_dim(acts, 1 - core, 0, keepdims=False)
    across = lambda flip: [(d * 32 + f, (1 - d) * 32 + (f ^ flip)) for d in range(2) for f in range(32)]
    other_mine = lax.ppermute(keep, ("dp", "feat"), across(0))
    other_theirs = lax.ppermute(send, ("dp", "feat"), across(1))
    own_theirs = lax.ppermute(send, "feat", PARTNER)
    w_mine = cut(at, dec_weight)
    w_theirs = lax.ppermute(w_mine, "feat", PARTNER)
    weights = (w_mine, w_theirs)
    def shift(array, by):
        return lax.ppermute(array, "layer", ring(by))

    both = jnp.stack([keep, own_theirs])
    up, down = shift(both, 1), shift(both, -1)
    up_mine = up[0]
    down_theirs = down[1]
    far = [shift(up_mine, 1), shift(down_theirs, -1)]
    near = [both, up, down]
    own = decode(at, weights, near, far)

    up_mine, down_mine = shift(other_mine, 1), shift(other_mine, -1)
    up_theirs, down_theirs = shift(other_theirs, 1), shift(other_theirs, -1)
    far = [shift(up_mine, 1), shift(down_theirs, -1)]
    near = [other_mine, other_theirs, up_mine, up_theirs, down_mine, down_theirs]
    other = decode(at, weights, near, far)

    chips = []
    for (kept, *away) in (own, other):
        came = []
        for by, piece in enumerate(away):
            came.append(lax.ppermute(piece, "feat", x_pairs(by + 1)))
        chips = [x_sum(at, chips, kept, came)]
    chips = lax.all_to_all(chips[0], "feat", 0, 0, tiled=True, axis_index_groups=ZC_GROUPS)
    out = finish(at, chips, dec_bias.reshape(36, 1))
    return out.T[None]


def solution(mesh):
    in_specs = (
        P("layer", "dp", None),
        P("layer", None, "feat"),
        P("layer", "feat"),
        P("layer", None, "feat", "dp"),
        P("layer", ("dp", "feat")),
        P("dp"),
    )
    out_specs = P("layer", None, ("dp", "feat"))


    return jax.shard_map(per_device, mesh=mesh, in_specs=in_specs, out_specs=out_specs, check_vma=False)
```

```python
import functools

import jax
import jax.numpy as jnp
from jax import lax
from jax.experimental import pallas as pl
from jax.experimental.pallas import tpu as pltpu
from jax.sharding import PartitionSpec as P


SEQ = 128
BF = jnp.bfloat16
F32 = jnp.float32

NX, NZ = 4, 4
PARTNER = [(i, i ^ 1) for i in range(32)]


def feat_at(z, x, c):
    return z * 8 + x * 2 + c


def x_pairs(by):
    return [
        (feat_at(z, x, c), feat_at(z, (x + by) % NX, c))
        for z in range(NZ) for x in range(NX) for c in range(2)
    ]


def ring(by):
    return [(i, (i + by) % 4) for i in range(4)]


ZC_GROUPS = [[feat_at(z, x, c) for z in range(NZ) for c in range(2)] for x in range(NX)]


IN_VMEM = pl.BlockSpec(memory_space=pltpu.VMEM)
IN_SMEM = pl.BlockSpec(memory_space=pltpu.SMEM)
MIB = 1 << 20


def call(kernel, out_shape, operands, grant, scratch=(), flops=0):
    single = not isinstance(out_shape, (list, tuple))
    moved = sum(a.size * a.dtype.itemsize for a in operands)
    return pl.pallas_call(
        kernel,
        out_shape=out_shape,
        in_specs=[IN_SMEM] + [IN_VMEM] * (len(operands) - 1),
        out_specs=IN_VMEM if single else [IN_VMEM] * len(out_shape),
        scratch_shapes=list(scratch),
        compiler_params=pltpu.CompilerParams(vmem_limit_bytes=grant * MIB),
        cost_estimate=pl.CostEstimate(flops=flops, bytes_accessed=moved, transcendentals=0),
    )(*operands)


TILES = (slice(0, 512), slice(512, 1024), slice(1024, 1152))
GRANT = 12
CUT_GRANT = 48


def terms_of(backs, weights, blocks, cols):
    total = None
    for i, block in enumerate(blocks):
        term = jnp.dot(block[...], weights[i % 2][backs[i // 2], :, cols], preferred_element_type=F32)
        total = term if total is None else total + term
    return total


def cut_kernel(at_ref, decoders_ref, out_ref, sems):
    target = at_ref[1]
    copies = [
        pltpu.make_async_copy(decoders_ref.at[0, jnp.maximum(target - back, 0)], out_ref.at[back], sems.at[back])
        for back in range(4)
    ]
    for copy in copies:
        copy.start()
    for back, copy in enumerate(copies):
        copy.wait()
        if back:

            @pl.when(target < back)
            def _(back=back):
                out_ref[back] = jnp.zeros_like(out_ref[back])


def cut(at, decoders):
    return pl.pallas_call(
        cut_kernel,
        out_shape=jax.ShapeDtypeStruct(decoders.shape[1:], BF),
        in_specs=[IN_SMEM, pl.BlockSpec(memory_space=pltpu.HBM)],
        out_specs=IN_VMEM,
        scratch_shapes=[pltpu.SemaphoreType.DMA((4,))],
        compiler_params=pltpu.CompilerParams(vmem_limit_bytes=CUT_GRANT * MIB),
        cost_estimate=pl.CostEstimate(flops=0, bytes_accessed=2 * decoders.size, transcendentals=0),
        name="cut",
    )(at, decoders)


def partial_kernel(backs, at_ref, *refs):
    weights, blocks, total_ref = refs[:2], refs[2:-1], refs[-1]
    for cols in TILES:
        total_ref[:, cols] = terms_of(backs, weights, blocks, cols)


def partial(at, weights, backs, blocks):
    rows, cols = blocks[0].shape[-2], weights[0].shape[2]
    return call(
        functools.partial(partial_kernel, backs),
        jax.ShapeDtypeStruct((rows, cols), F32),
        [at, *weights, *blocks], GRANT, flops=4 * len(backs) * rows * 512 * cols,
    )


def last_kernel(backs, has_base, at_ref, *refs):
    weights, refs = refs[:2], refs[2:]
    turned = refs[-1]
    self_ref, *away = refs[-5:-1]
    refs = refs[:-5]
    blocks = refs[has_base:]
    for cols in TILES:
        total = terms_of(backs, weights, blocks, cols)
        if has_base:
            total = total + refs[0][:, cols]
        turned[cols, :] = total.T
    for by in range(NX):
        owner = lax.rem(at_ref[2] + by, NX)
        for z in range(NZ):
            piece = turned[pl.ds(pl.multiple_of((z * NX + owner) * 72, 8), 72), :]
            if by == 0:
                self_ref[z] = piece
            else:
                away[by - 1][z] = piece.astype(BF)


def last(at, weights, base, backs, blocks):
    rows, cols = blocks[0].shape[-2], weights[0].shape[2]
    piece = (NZ, cols // (NX * NZ), rows)
    return call(
        functools.partial(last_kernel, backs, len(base)),
        [jax.ShapeDtypeStruct(piece, F32)] + [jax.ShapeDtypeStruct(piece, BF)] * 3,
        [at, *weights, *base, *blocks], GRANT,
        scratch=[pltpu.VMEM((cols, rows), F32)], flops=4 * len(backs) * rows * 512 * cols,
    )


def decode(at, weights, near, far):
    total = partial(at, weights, (0, 1, 3), near)
    return last(at, weights, [total], (2,), far)


def x_sum_kernel(at_ref, *refs):
    *before, self_ref, a_ref, b_ref, c_ref, out_ref = refs
    for z in range(NZ):
        total = self_ref[z] + a_ref[z].astype(F32) + b_ref[z].astype(F32) + c_ref[z].astype(F32)
        total = total.astype(BF)
        for c, piece in enumerate((total[:36], total[36:])):
            if before:
                out_ref[2 * z + c, :36] = before[0][2 * z + c]
                out_ref[2 * z + c, 36:] = piece
            else:
                out_ref[2 * z + c] = piece


def x_sum(at, before, kept, came):
    shape = (2 * NZ, 72 if before else 36, 256)
    return call(x_sum_kernel, jax.ShapeDtypeStruct(shape, BF), [at, *before, kept, *came], 8)


def final_kernel(at_ref, chips_ref, bias_ref, out_ref):
    for c in range(2):
        chips = chips_ref[c].astype(F32)
        for z in range(1, NZ):
            chips = chips + chips_ref[2 * z + c].astype(F32)
        for block in range(2):
            total = (chips[block * 36 : (block + 1) * 36] + bias_ref[...]).astype(BF)
            for dp in range(2):

                @pl.when(at_ref[3] == dp)
                def _(total=total, start=(dp ^ block) * 512 + c * 256):
                    out_ref[:, start : start + 256] = total


def finish(at, chips, bias):
    return call(final_kernel, jax.ShapeDtypeStruct((36, 1024), BF), [at, chips, bias], 8)


def per_device(resid, enc_weight, enc_bias, dec_weight, dec_bias, lengths):
    target, feat, dp = lax.axis_index("layer"), lax.axis_index("feat"), lax.axis_index("dp")
    core = feat % 2
    at = jnp.stack([core, target, feat // 2 % NX, dp]).astype(jnp.int32)
    valid = (jnp.arange(SEQ)[None, :] < lengths[:, None]).reshape(-1).astype(F32)
    pre = jnp.dot(resid[0], enc_weight[0], preferred_element_type=F32) + enc_bias
    acts = (jax.nn.relu(pre) * valid[:, None]).astype(BF).reshape(2, 256, 512)
    keep = lax.dynamic_index_in_dim(acts, core, 0, keepdims=False)
    send = lax.dynamic_index_in_dim(acts, 1 - core, 0, keepdims=False)
    across = lambda flip: [(d * 32 + f, (1 - d) * 32 + (f ^ flip)) for d in range(2) for f in range(32)]
    other_mine = lax.ppermute(keep, ("dp", "feat"), across(0))
    other_theirs = lax.ppermute(send, ("dp", "feat"), across(1))
    own_theirs = lax.ppermute(send, "feat", PARTNER)
    w_mine = cut(at, dec_weight)
    w_theirs = lax.ppermute(w_mine, "feat", PARTNER)
    weights = (w_mine, w_theirs)
    def shift(array, by):
        return lax.ppermute(array, "layer", ring(by))

    blocks = {}
    for name, mine, theirs in (("own", keep, own_theirs), ("other", other_mine, other_theirs)):
        up_mine, down_mine = shift(mine, 1), shift(mine, -1)
        up_theirs, down_theirs = shift(theirs, 1), shift(theirs, -1)
        onward = up_mine, down_theirs
        if name == "own":
            ahead = jnp.maximum(up_mine, 0)
            onward = ahead, jnp.maximum(down_theirs, 0)
        far = [shift(onward[0], 1), shift(onward[1], -1)]
        near = [mine, theirs, up_mine, up_theirs, down_mine, down_theirs]
        blocks[name] = decode(at, weights, near, far)

    chips = []
    for (kept, *away) in blocks.values():
        came = []
        for by, piece in enumerate(away):
            came.append(lax.ppermute(piece, "feat", x_pairs(by + 1)))
        chips = [x_sum(at, chips, kept, came)]
    chips = lax.all_to_all(chips[0], "feat", 0, 0, tiled=True, axis_index_groups=ZC_GROUPS)
    out = finish(at, chips, dec_bias.reshape(36, 1))
    return out.T[None]


def solution(mesh):
    in_specs = (
        P("layer", "dp", None),
        P("layer", None, "feat"),
        P("layer", "feat"),
        P("layer", None, "feat", "dp"),
        P("layer", ("dp", "feat")),
        P("dp"),
    )
    out_specs = P("layer", None, ("dp", "feat"))


    return jax.shard_map(per_device, mesh=mesh, in_specs=in_specs, out_specs=out_specs, check_vma=False)
```

```python
import functools

import jax
import jax.numpy as jnp
from jax import lax
from jax.experimental import pallas as pl
from jax.experimental.pallas import tpu as pltpu
from jax.sharding import PartitionSpec as P


SEQ = 128
BF = jnp.bfloat16
F32 = jnp.float32

NX, NZ = 4, 4
PARTNER = [(i, i ^ 1) for i in range(32)]


def feat_at(z, x, c):
    return z * 8 + x * 2 + c


def x_pairs(by):
    return [
        (feat_at(z, x, c), feat_at(z, (x + by) % NX, c))
        for z in range(NZ) for x in range(NX) for c in range(2)
    ]


def ring(by):
    return [(i, (i + by) % 4) for i in range(4)]


ZC_GROUPS = [[feat_at(z, x, c) for z in range(NZ) for c in range(2)] for x in range(NX)]


IN_VMEM = pl.BlockSpec(memory_space=pltpu.VMEM)
IN_SMEM = pl.BlockSpec(memory_space=pltpu.SMEM)
MIB = 1 << 20


def call(kernel, out_shape, operands, grant, scratch=(), flops=0):
    single = not isinstance(out_shape, (list, tuple))
    moved = sum(a.size * a.dtype.itemsize for a in operands)
    return pl.pallas_call(
        kernel,
        out_shape=out_shape,
        in_specs=[IN_SMEM] + [IN_VMEM] * (len(operands) - 1),
        out_specs=IN_VMEM if single else [IN_VMEM] * len(out_shape),
        scratch_shapes=list(scratch),
        compiler_params=pltpu.CompilerParams(vmem_limit_bytes=grant * MIB),
        cost_estimate=pl.CostEstimate(flops=flops, bytes_accessed=moved, transcendentals=0),
    )(*operands)


TILES = (slice(0, 512), slice(512, 1024), slice(1024, 1152))
GRANT = 12
CUT_GRANT = 48


def terms_of(backs, weights, blocks, cols):
    total = None
    for i, block in enumerate(blocks):
        term = jnp.dot(block[...], weights[i % 2][backs[i // 2], :, cols], preferred_element_type=F32)
        total = term if total is None else total + term
    return total


def cut_kernel(at_ref, decoders_ref, out_ref, sems):
    target = at_ref[1]
    copies = [
        pltpu.make_async_copy(decoders_ref.at[0, jnp.maximum(target - back, 0)], out_ref.at[back], sems.at[back])
        for back in range(4)
    ]
    for copy in copies:
        copy.start()
    for back, copy in enumerate(copies):
        copy.wait()
        if back:

            @pl.when(target < back)
            def _(back=back):
                out_ref[back] = jnp.zeros_like(out_ref[back])


def cut(at, decoders):
    return pl.pallas_call(
        cut_kernel,
        out_shape=jax.ShapeDtypeStruct(decoders.shape[1:], BF),
        in_specs=[IN_SMEM, pl.BlockSpec(memory_space=pltpu.HBM)],
        out_specs=IN_VMEM,
        scratch_shapes=[pltpu.SemaphoreType.DMA((4,))],
        compiler_params=pltpu.CompilerParams(vmem_limit_bytes=CUT_GRANT * MIB),
        cost_estimate=pl.CostEstimate(flops=0, bytes_accessed=2 * decoders.size, transcendentals=0),
        name="cut",
    )(at, decoders)


def partial_kernel(backs, at_ref, *refs):
    weights, blocks, total_ref = refs[:2], refs[2:-1], refs[-1]
    for cols in TILES:
        total_ref[:, cols] = terms_of(backs, weights, blocks, cols)


def partial(at, weights, backs, blocks):
    rows, cols = blocks[0].shape[-2], weights[0].shape[2]
    return call(
        functools.partial(partial_kernel, backs),
        jax.ShapeDtypeStruct((rows, cols), F32),
        [at, *weights, *blocks], GRANT, flops=4 * len(backs) * rows * 512 * cols,
    )


def last_kernel(backs, has_base, at_ref, *refs):
    weights, refs = refs[:2], refs[2:]
    turned = refs[-1]
    self_ref, *away = refs[-5:-1]
    refs = refs[:-5]
    blocks = refs[has_base:]
    for cols in TILES:
        total = terms_of(backs, weights, blocks, cols)
        if has_base:
            total = total + refs[0][:, cols]
        turned[cols, :] = total.T
    for by in range(NX):
        owner = lax.rem(at_ref[2] + by, NX)
        for z in range(NZ):
            piece = turned[pl.ds(pl.multiple_of((z * NX + owner) * 72, 8), 72), :]
            if by == 0:
                self_ref[z] = piece
            else:
                away[by - 1][z] = piece.astype(BF)


def last(at, weights, base, backs, blocks):
    rows, cols = blocks[0].shape[-2], weights[0].shape[2]
    piece = (NZ, cols // (NX * NZ), rows)
    return call(
        functools.partial(last_kernel, backs, len(base)),
        [jax.ShapeDtypeStruct(piece, F32)] + [jax.ShapeDtypeStruct(piece, BF)] * 3,
        [at, *weights, *base, *blocks], GRANT,
        scratch=[pltpu.VMEM((cols, rows), F32)], flops=4 * len(backs) * rows * 512 * cols,
    )


def decode(at, weights, near, far):
    total = partial(at, weights, (0, 1, 3), near)
    return last(at, weights, [total], (2,), far)


def x_sum_kernel(at_ref, *refs):
    *before, self_ref, a_ref, b_ref, c_ref, out_ref = refs
    for z in range(NZ):
        total = self_ref[z] + a_ref[z].astype(F32) + b_ref[z].astype(F32) + c_ref[z].astype(F32)
        total = total.astype(BF)
        for c, piece in enumerate((total[:36], total[36:])):
            if before:
                out_ref[2 * z + c, :36] = before[0][2 * z + c]
                out_ref[2 * z + c, 36:] = piece
            else:
                out_ref[2 * z + c] = piece


def x_sum(at, before, kept, came):
    shape = (2 * NZ, 72 if before else 36, 256)
    return call(x_sum_kernel, jax.ShapeDtypeStruct(shape, BF), [at, *before, kept, *came], 8)


def final_kernel(at_ref, chips_ref, bias_ref, out_ref):
    for c in range(2):
        chips = chips_ref[c].astype(F32)
        for z in range(1, NZ):
            chips = chips + chips_ref[2 * z + c].astype(F32)
        for block in range(2):
            total = (chips[block * 36 : (block + 1) * 36] + bias_ref[...]).astype(BF)
            for dp in range(2):

                @pl.when(at_ref[3] == dp)
                def _(total=total, start=(dp ^ block) * 512 + c * 256):
                    out_ref[:, start : start + 256] = total


def finish(at, chips, bias):
    return call(final_kernel, jax.ShapeDtypeStruct((36, 1024), BF), [at, chips, bias], 8)


def per_device(resid, enc_weight, enc_bias, dec_weight, dec_bias, lengths):
    target, feat, dp = lax.axis_index("layer"), lax.axis_index("feat"), lax.axis_index("dp")
    core = feat % 2
    at = jnp.stack([core, target, feat // 2 % NX, dp]).astype(jnp.int32)

    def encode(half):
        rows = lax.dynamic_index_in_dim(resid[0].reshape(2, 256, 2304), half, 0, keepdims=False)
        first, second = (lax.dynamic_index_in_dim(lengths, 2 * half + s, keepdims=False) for s in range(2))
        pre = jnp.dot(rows, enc_weight[0], preferred_element_type=F32) + enc_bias
        row = lax.broadcasted_iota(jnp.int32, pre.shape, 0)
        limit = jnp.where(row < SEQ, first, SEQ + second)
        return jnp.where(row < limit, jax.nn.relu(pre), 0.0).astype(BF)

    keep = encode(core)
    send = encode(1 - core)
    across = lambda flip: [(d * 32 + f, (1 - d) * 32 + (f ^ flip)) for d in range(2) for f in range(32)]
    other_mine = lax.ppermute(keep, ("dp", "feat"), across(0))
    other_theirs = lax.ppermute(send, ("dp", "feat"), across(1))
    own_theirs = lax.ppermute(send, "feat", PARTNER)
    w_mine = cut(at, dec_weight)
    w_theirs = lax.ppermute(w_mine, "feat", PARTNER)
    weights = (w_mine, w_theirs)

    def shift(array, by):
        return lax.ppermute(array, "layer", ring(by))

    blocks = {}
    for name, mine, theirs in (("own", keep, own_theirs), ("other", other_mine, other_theirs)):
        up_mine, down_mine = shift(mine, 1), shift(mine, -1)
        up_theirs, down_theirs = shift(theirs, 1), shift(theirs, -1)
        onward = up_mine, down_theirs
        if name == "own":
            ahead = jnp.maximum(up_mine, 0)
            onward = ahead, jnp.maximum(down_theirs, 0)
        far = [shift(onward[0], 1), shift(onward[1], -1)]
        near = [mine, theirs, up_mine, up_theirs, down_mine, down_theirs]
        blocks[name] = decode(at, weights, near, far)

    chips = []
    for (kept, *away) in blocks.values():
        came = []
        for by, piece in enumerate(away):
            came.append(lax.ppermute(piece, "feat", x_pairs(by + 1)))
        chips = [x_sum(at, chips, kept, came)]
    chips = lax.all_to_all(chips[0], "feat", 0, 0, tiled=True, axis_index_groups=ZC_GROUPS)
    out = finish(at, chips, dec_bias.reshape(36, 1))
    return out.T[None]


def solution(mesh):
    in_specs = (
        P("layer", "dp", None),
        P("layer", None, "feat"),
        P("layer", "feat"),
        P("layer", None, "feat", "dp"),
        P("layer", ("dp", "feat")),
        P("dp"),
    )
    out_specs = P("layer", None, ("dp", "feat"))


    return jax.shard_map(per_device, mesh=mesh, in_specs=in_specs, out_specs=out_specs, check_vma=False)
```

```python
import functools

import jax
import jax.numpy as jnp
from jax import lax
from jax.experimental import pallas as pl
from jax.experimental.pallas import tpu as pltpu
from jax.sharding import PartitionSpec as P


SEQ = 128
BF = jnp.bfloat16
F32 = jnp.float32

NX, NZ = 4, 4
PARTNER = [(i, i ^ 1) for i in range(32)]


def feat_at(z, x, c):
    return z * 8 + x * 2 + c


def x_pairs(by):
    return [
        (feat_at(z, x, c), feat_at(z, (x + by) % NX, c))
        for z in range(NZ) for x in range(NX) for c in range(2)
    ]


def ring(by):
    return [(i, (i + by) % 4) for i in range(4)]


def z_pairs(k):
    return [
        (feat_at(z, x, c), feat_at(z ^ k, x, c))
        for z in range(NZ) for x in range(NX) for c in range(2)
    ]


IN_VMEM = pl.BlockSpec(memory_space=pltpu.VMEM)
IN_SMEM = pl.BlockSpec(memory_space=pltpu.SMEM)
MIB = 1 << 20


def call(kernel, out_shape, operands, grant, scratch=(), flops=0):
    single = not isinstance(out_shape, (list, tuple))
    moved = sum(a.size * a.dtype.itemsize for a in operands)
    return pl.pallas_call(
        kernel,
        out_shape=out_shape,
        in_specs=[IN_SMEM] + [IN_VMEM] * (len(operands) - 1),
        out_specs=IN_VMEM if single else [IN_VMEM] * len(out_shape),
        scratch_shapes=list(scratch),
        compiler_params=pltpu.CompilerParams(vmem_limit_bytes=grant * MIB),
        cost_estimate=pl.CostEstimate(flops=flops, bytes_accessed=moved, transcendentals=0),
    )(*operands)


TILES = (slice(0, 512), slice(512, 1024), slice(1024, 1152))
GRANT = 12
CUT_GRANT = 48


def terms_of(backs, weights, blocks, cols):
    total = None
    for i, block in enumerate(blocks):
        term = jnp.dot(block[...], weights[i % 2][backs[i // 2], :, cols], preferred_element_type=F32)
        total = term if total is None else total + term
    return total


def cut_kernel(at_ref, decoders_ref, out_ref, sems):
    target = at_ref[1]
    copies = [
        pltpu.make_async_copy(decoders_ref.at[0, jnp.maximum(target - back, 0)], out_ref.at[back], sems.at[back])
        for back in range(4)
    ]
    for copy in copies:
        copy.start()
    for back, copy in enumerate(copies):
        copy.wait()
        if back:

            @pl.when(target < back)
            def _(back=back):
                out_ref[back] = jnp.zeros_like(out_ref[back])


def cut(at, decoders):
    return pl.pallas_call(
        cut_kernel,
        out_shape=jax.ShapeDtypeStruct(decoders.shape[1:], BF),
        in_specs=[IN_SMEM, pl.BlockSpec(memory_space=pltpu.HBM)],
        out_specs=IN_VMEM,
        scratch_shapes=[pltpu.SemaphoreType.DMA((4,))],
        compiler_params=pltpu.CompilerParams(vmem_limit_bytes=CUT_GRANT * MIB),
        cost_estimate=pl.CostEstimate(flops=0, bytes_accessed=2 * decoders.size, transcendentals=0),
        name="cut",
    )(at, decoders)


def partial_kernel(backs, at_ref, *refs):
    weights, blocks, total_ref = refs[:2], refs[2:-1], refs[-1]
    for cols in TILES:
        total_ref[:, cols] = terms_of(backs, weights, blocks, cols)


def partial(at, weights, backs, blocks):
    rows, cols = blocks[0].shape[-2], weights[0].shape[2]
    return call(
        functools.partial(partial_kernel, backs),
        jax.ShapeDtypeStruct((rows, cols), F32),
        [at, *weights, *blocks], GRANT, flops=4 * len(backs) * rows * 512 * cols,
    )


def last_kernel(backs, has_base, at_ref, *refs):
    weights, refs = refs[:2], refs[2:]
    turned = refs[-1]
    self_ref, *away = refs[-5:-1]
    refs = refs[:-5]
    blocks = refs[has_base:]
    for cols in TILES:
        total = terms_of(backs, weights, blocks, cols)
        if has_base:
            total = total + refs[0][:, cols]
        turned[cols, :] = total.T
    for by in range(NX):
        owner = lax.rem(at_ref[2] + by, NX)
        for z in range(NZ):
            piece = turned[pl.ds(pl.multiple_of((z * NX + owner) * 72, 8), 72), :]
            if by == 0:
                self_ref[z] = piece
            else:
                away[by - 1][z] = piece.astype(BF)


def last(at, weights, base, backs, blocks):
    rows, cols = blocks[0].shape[-2], weights[0].shape[2]
    piece = (NZ, cols // (NX * NZ), rows)
    return call(
        functools.partial(last_kernel, backs, len(base)),
        [jax.ShapeDtypeStruct(piece, F32)] + [jax.ShapeDtypeStruct(piece, BF)] * 3,
        [at, *weights, *base, *blocks], GRANT,
        scratch=[pltpu.VMEM((cols, rows), F32)], flops=4 * len(backs) * rows * 512 * cols,
    )


def decode(at, weights, near, far):
    total = partial(at, weights, (0, 1, 3), near)
    return last(at, weights, [total], (2,), far)


def x_total(refs, z):
    self_ref, a_ref, b_ref, c_ref = refs
    return self_ref[z] + a_ref[z].astype(F32) + b_ref[z].astype(F32) + c_ref[z].astype(F32)


def x_sum_kernel(at_ref, *refs):
    for z in range(NZ):
        refs[-1][z] = x_total(refs[:-1], z)


def x_sum(at, kept, came):
    return call(x_sum_kernel, jax.ShapeDtypeStruct(kept.shape, F32), [at, kept, *came], 8)


def x_cut_kernel(at_ref, before_ref, *refs):
    for k, out_ref in enumerate(refs[4:]):
        z = at_ref[4] ^ k
        out_ref[0] = before_ref[z].astype(out_ref.dtype)
        out_ref[1] = x_total(refs[:4], z).astype(out_ref.dtype)


def x_cut(at, before, kept, came):
    shape = (2, *kept.shape[1:])
    out = [jax.ShapeDtypeStruct(shape, F32)] + [jax.ShapeDtypeStruct(shape, BF)] * 3
    return call(x_cut_kernel, out, [at, before, kept, *came], 8)


def z_sum_kernel(at_ref, kept_ref, a_ref, b_ref, c_ref, mine_ref, away_ref):
    total = kept_ref[...] + a_ref[...].astype(F32) + b_ref[...].astype(F32) + c_ref[...].astype(F32)
    low, high = total[:, :36], total[:, 36:]
    for core, (mine, away) in enumerate(((low, high), (high, low))):

        @pl.when(at_ref[0] == core)
        def _(mine=mine, away=away):
            mine_ref[...] = mine
            away_ref[...] = away


def z_sum(at, kept, came):
    out = [jax.ShapeDtypeStruct((2, 36, 256), F32)] * 2
    return call(z_sum_kernel, out, [at, kept, *came], 8)


def final_kernel(at_ref, mine_ref, came_ref, bias_ref, out_ref):
    for core in range(2):
        for dp in range(2):

            @pl.when((at_ref[0] == core) & (at_ref[3] == dp))
            def _(core=core, dp=dp):
                for ref, half in ((mine_ref, core), (came_ref, 1 - core)):
                    for block in range(2):
                        start = (dp ^ block) * 512 + half * 256
                        out_ref[:, start : start + 256] = (ref[block] + bias_ref[...]).astype(BF)


def finish(at, mine, came, bias):
    return call(final_kernel, jax.ShapeDtypeStruct((36, 1024), BF), [at, mine, came, bias], 8)


def per_device(resid, enc_weight, enc_bias, dec_weight, dec_bias, lengths):
    target, feat, dp = lax.axis_index("layer"), lax.axis_index("feat"), lax.axis_index("dp")
    core = feat % 2
    at = jnp.stack([core, target, feat // 2 % NX, dp, feat // 8]).astype(jnp.int32)
    valid = (jnp.arange(SEQ)[None, :] < lengths[:, None]).reshape(-1).astype(F32)
    pre = jnp.dot(resid[0], enc_weight[0], preferred_element_type=F32) + enc_bias
    acts = (jax.nn.relu(pre) * valid[:, None]).astype(BF).reshape(2, 256, 512)
    keep = lax.dynamic_index_in_dim(acts, core, 0, keepdims=False)
    send = lax.dynamic_index_in_dim(acts, 1 - core, 0, keepdims=False)
    across = lambda flip: [(d * 32 + f, (1 - d) * 32 + (f ^ flip)) for d in range(2) for f in range(32)]
    other_mine = lax.ppermute(keep, ("dp", "feat"), across(0))
    other_theirs = lax.ppermute(send, ("dp", "feat"), across(1))
    own_theirs = lax.ppermute(send, "feat", PARTNER)
    w_mine = cut(at, dec_weight)
    w_theirs = lax.ppermute(w_mine, "feat", PARTNER)
    weights = (w_mine, w_theirs)
    def shift(array, by):
        return lax.ppermute(array, "layer", ring(by))

    blocks = {}
    for name, mine, theirs in (("own", keep, own_theirs), ("other", other_mine, other_theirs)):
        up_mine, down_mine = shift(mine, 1), shift(mine, -1)
        up_theirs, down_theirs = shift(theirs, 1), shift(theirs, -1)
        onward = up_mine, down_theirs
        if name == "own":
            ahead = jnp.maximum(up_mine, 0)
            onward = ahead, jnp.maximum(down_theirs, 0)
        far = [shift(onward[0], 1), shift(onward[1], -1)]
        near = [mine, theirs, up_mine, up_theirs, down_mine, down_theirs]
        blocks[name] = decode(at, weights, near, far)

    for name, (kept, *away) in blocks.items():
        came = []
        for by, piece in enumerate(away):
            came.append(lax.ppermute(piece, "feat", x_pairs(by + 1)))
        if name == "own":
            before = x_sum(at, kept, came)
        else:
            kept, *away = x_cut(at, before, kept, came)
    came = []
    for k in (3, 2, 1):
        came.append(lax.ppermute(away[k - 1], "feat", z_pairs(k)))
    mine, away = z_sum(at, kept, came)
    came = lax.ppermute(away, "feat", PARTNER)
    out = finish(at, mine, came, dec_bias.reshape(36, 1))
    return out.T[None]


def solution(mesh):
    in_specs = (
        P("layer", "dp", None),
        P("layer", None, "feat"),
        P("layer", "feat"),
        P("layer", None, "feat", "dp"),
        P("layer", ("dp", "feat")),
        P("dp"),
    )
    out_specs = P("layer", None, ("dp", "feat"))


    return jax.shard_map(per_device, mesh=mesh, in_specs=in_specs, out_specs=out_specs, check_vma=False)
```

```python
import functools

import jax
import jax.numpy as jnp
from jax import lax
from jax.experimental import pallas as pl
from jax.experimental.pallas import tpu as pltpu
from jax.sharding import PartitionSpec as P


SEQ = 128
BF = jnp.bfloat16
F32 = jnp.float32

NX, NZ = 4, 4
PARTNER = [(i, i ^ 1) for i in range(32)]


def feat_at(z, x, c):
    return z * 8 + x * 2 + c


def x_pairs(by):
    return [
        (feat_at(z, x, c), feat_at(z, (x + by) % NX, c))
        for z in range(NZ) for x in range(NX) for c in range(2)
    ]


def ring(by):
    return [(i, (i + by) % 4) for i in range(4)]


def z_pairs(k):
    return [
        (feat_at(z, x, c), feat_at(z ^ k, x, c))
        for z in range(NZ) for x in range(NX) for c in range(2)
    ]


IN_VMEM = pl.BlockSpec(memory_space=pltpu.VMEM)
IN_SMEM = pl.BlockSpec(memory_space=pltpu.SMEM)
MIB = 1 << 20


def call(kernel, out_shape, operands, grant, scratch=(), flops=0):
    single = not isinstance(out_shape, (list, tuple))
    moved = sum(a.size * a.dtype.itemsize for a in operands)
    return pl.pallas_call(
        kernel,
        out_shape=out_shape,
        in_specs=[IN_SMEM] + [IN_VMEM] * (len(operands) - 1),
        out_specs=IN_VMEM if single else [IN_VMEM] * len(out_shape),
        scratch_shapes=list(scratch),
        compiler_params=pltpu.CompilerParams(vmem_limit_bytes=grant * MIB),
        cost_estimate=pl.CostEstimate(flops=flops, bytes_accessed=moved, transcendentals=0),
    )(*operands)


TILES = (slice(0, 512), slice(512, 1024), slice(1024, 1152))
GRANT = 12
CUT_GRANT = 48


def terms_of(backs, weights, blocks, cols):
    total = None
    for i, block in enumerate(blocks):
        term = jnp.dot(block[...], weights[i % 2][backs[i // 2], :, cols], preferred_element_type=F32)
        total = term if total is None else total + term
    return total


def cut_kernel(at_ref, decoders_ref, out_ref, sems):
    target = at_ref[1]
    copies = [
        pltpu.make_async_copy(decoders_ref.at[0, jnp.maximum(target - back, 0)], out_ref.at[back], sems.at[back])
        for back in range(4)
    ]
    for copy in copies:
        copy.start()
    for back, copy in enumerate(copies):
        copy.wait()
        if back:

            @pl.when(target < back)
            def _(back=back):
                out_ref[back] = jnp.zeros_like(out_ref[back])


def cut(at, decoders):
    return pl.pallas_call(
        cut_kernel,
        out_shape=jax.ShapeDtypeStruct(decoders.shape[1:], BF),
        in_specs=[IN_SMEM, pl.BlockSpec(memory_space=pltpu.HBM)],
        out_specs=IN_VMEM,
        scratch_shapes=[pltpu.SemaphoreType.DMA((4,))],
        compiler_params=pltpu.CompilerParams(vmem_limit_bytes=CUT_GRANT * MIB),
        cost_estimate=pl.CostEstimate(flops=0, bytes_accessed=2 * decoders.size, transcendentals=0),
        name="cut",
    )(at, decoders)


def partial_kernel(backs, at_ref, *refs):
    weights, blocks, total_ref = refs[:2], refs[2:-1], refs[-1]
    for cols in TILES:
        total_ref[:, cols] = terms_of(backs, weights, blocks, cols)


def partial(at, weights, backs, blocks):
    rows, cols = blocks[0].shape[-2], weights[0].shape[2]
    return call(
        functools.partial(partial_kernel, backs),
        jax.ShapeDtypeStruct((rows, cols), F32),
        [at, *weights, *blocks], GRANT, flops=4 * len(backs) * rows * 512 * cols,
    )


def last_kernel(backs, has_base, at_ref, *refs):
    weights, refs = refs[:2], refs[2:]
    turned = refs[-1]
    self_ref, *away = refs[-5:-1]
    refs = refs[:-5]
    blocks = refs[has_base:]
    for cols in TILES:
        total = terms_of(backs, weights, blocks, cols)
        if has_base:
            total = total + refs[0][:, cols]
        turned[cols, :] = total.T
    for by in range(NX):
        owner = lax.rem(at_ref[2] + by, NX)
        for z in range(NZ):
            piece = turned[pl.ds(pl.multiple_of((z * NX + owner) * 72, 8), 72), :]
            if by == 0:
                self_ref[z] = piece
            else:
                away[by - 1][z] = piece.astype(BF)


def last(at, weights, base, backs, blocks):
    rows, cols = blocks[0].shape[-2], weights[0].shape[2]
    piece = (NZ, cols // (NX * NZ), rows)
    return call(
        functools.partial(last_kernel, backs, len(base)),
        [jax.ShapeDtypeStruct(piece, F32)] + [jax.ShapeDtypeStruct(piece, BF)] * 3,
        [at, *weights, *base, *blocks], GRANT,
        scratch=[pltpu.VMEM((cols, rows), F32)], flops=4 * len(backs) * rows * 512 * cols,
    )


def decode(at, weights, near, far):
    total = partial(at, weights, (0, 1, 3), near)
    return last(at, weights, [total], (2,), far)


def x_total(refs, z):
    self_ref, a_ref, b_ref, c_ref = refs
    return self_ref[z] + a_ref[z].astype(F32) + b_ref[z].astype(F32) + c_ref[z].astype(F32)


def x_cut_kernel(at_ref, *refs):
    for k, out_ref in enumerate(refs[4:]):
        out_ref[...] = x_total(refs[:4], at_ref[4] ^ k).astype(out_ref.dtype)


def x_cut(at, kept, came):
    shape = kept.shape[1:]
    out = [jax.ShapeDtypeStruct(shape, F32)] + [jax.ShapeDtypeStruct(shape, BF)] * 3
    return call(x_cut_kernel, out, [at, kept, *came], 8)


def z_sum_kernel(at_ref, *refs):
    mine_ref, away_ref = refs[-2:]
    for block in range(2):
        kept_ref, a_ref, b_ref, c_ref = refs[4 * block : 4 * block + 4]
        total = kept_ref[...] + a_ref[...].astype(F32) + b_ref[...].astype(F32) + c_ref[...].astype(F32)
        low, high = total[:36], total[36:]
        for core, (mine, away) in enumerate(((low, high), (high, low))):

            @pl.when(at_ref[0] == core)
            def _(mine=mine, away=away, block=block):
                mine_ref[block] = mine
                away_ref[block] = away


def z_sum(at, pieces):
    out = [jax.ShapeDtypeStruct((2, 36, 256), F32)] * 2
    return call(z_sum_kernel, out, [at, *pieces], 8)


def final_kernel(at_ref, mine_ref, came_ref, bias_ref, out_ref):
    for core in range(2):
        for dp in range(2):

            @pl.when((at_ref[0] == core) & (at_ref[3] == dp))
            def _(core=core, dp=dp):
                for ref, half in ((mine_ref, core), (came_ref, 1 - core)):
                    for block in range(2):
                        start = (dp ^ block) * 512 + half * 256
                        out_ref[:, start : start + 256] = (ref[block] + bias_ref[...]).astype(BF)


def finish(at, mine, came, bias):
    return call(final_kernel, jax.ShapeDtypeStruct((36, 1024), BF), [at, mine, came, bias], 8)


def per_device(resid, enc_weight, enc_bias, dec_weight, dec_bias, lengths):
    target, feat, dp = lax.axis_index("layer"), lax.axis_index("feat"), lax.axis_index("dp")
    core = feat % 2
    at = jnp.stack([core, target, feat // 2 % NX, dp, feat // 8]).astype(jnp.int32)
    valid = (jnp.arange(SEQ)[None, :] < lengths[:, None]).reshape(-1).astype(F32)
    pre = jnp.dot(resid[0], enc_weight[0], preferred_element_type=F32) + enc_bias
    acts = (jax.nn.relu(pre) * valid[:, None]).astype(BF).reshape(2, 256, 512)
    keep = lax.dynamic_index_in_dim(acts, core, 0, keepdims=False)
    send = lax.dynamic_index_in_dim(acts, 1 - core, 0, keepdims=False)
    across = lambda flip: [(d * 32 + f, (1 - d) * 32 + (f ^ flip)) for d in range(2) for f in range(32)]
    other_mine = lax.ppermute(keep, ("dp", "feat"), across(0))
    other_theirs = lax.ppermute(send, ("dp", "feat"), across(1))
    own_theirs = lax.ppermute(send, "feat", PARTNER)
    w_mine = cut(at, dec_weight)
    w_theirs = lax.ppermute(w_mine, "feat", PARTNER)
    weights = (w_mine, w_theirs)
    def shift(array, by):
        return lax.ppermute(array, "layer", ring(by))

    blocks = {}
    for name, mine, theirs in (("own", keep, own_theirs), ("other", other_mine, other_theirs)):
        up_mine, down_mine = shift(mine, 1), shift(mine, -1)
        up_theirs, down_theirs = shift(theirs, 1), shift(theirs, -1)
        onward = up_mine, down_theirs
        if name == "own":
            ahead = jnp.maximum(up_mine, 0)
            onward = ahead, jnp.maximum(down_theirs, 0)
        far = [shift(onward[0], 1), shift(onward[1], -1)]
        near = [mine, theirs, up_mine, up_theirs, down_mine, down_theirs]
        blocks[name] = decode(at, weights, near, far)

    pieces = []
    for (kept, *away) in blocks.values():
        came = []
        for by, piece in enumerate(away):
            came.append(lax.ppermute(piece, "feat", x_pairs(by + 1)))
        kept, *away = x_cut(at, kept, came)
        pieces.append(kept)
        for k in (3, 2, 1):
            pieces.append(lax.ppermute(away[k - 1], "feat", z_pairs(k)))
    mine, away = z_sum(at, pieces)
    came = lax.ppermute(away, "feat", PARTNER)
    out = finish(at, mine, came, dec_bias.reshape(36, 1))
    return out.T[None]


def solution(mesh):
    in_specs = (
        P("layer", "dp", None),
        P("layer", None, "feat"),
        P("layer", "feat"),
        P("layer", None, "feat", "dp"),
        P("layer", ("dp", "feat")),
        P("dp"),
    )
    out_specs = P("layer", None, ("dp", "feat"))


    return jax.shard_map(per_device, mesh=mesh, in_specs=in_specs, out_specs=out_specs, check_vma=False)
```

```python
import functools

import jax
import jax.numpy as jnp
from jax import lax
from jax.experimental import pallas as pl
from jax.experimental.pallas import tpu as pltpu
from jax.sharding import PartitionSpec as P


SEQ = 128
BF = jnp.bfloat16
F32 = jnp.float32

NX, NZ = 4, 4
PARTNER = [(i, i ^ 1) for i in range(32)]


def feat_at(z, x, c):
    return z * 8 + x * 2 + c


def x_pairs(by):
    return [
        (feat_at(z, x, c), feat_at(z, (x + by) % NX, c))
        for z in range(NZ) for x in range(NX) for c in range(2)
    ]


def ring(by):
    return [(i, (i + by) % 4) for i in range(4)]


def z_pairs(k):
    return [
        (feat_at(z, x, c), feat_at(z ^ k, x, c))
        for z in range(NZ) for x in range(NX) for c in range(2)
    ]


IN_VMEM = pl.BlockSpec(memory_space=pltpu.VMEM)
IN_SMEM = pl.BlockSpec(memory_space=pltpu.SMEM)
MIB = 1 << 20


def call(kernel, out_shape, operands, grant, scratch=(), flops=0):
    single = not isinstance(out_shape, (list, tuple))
    moved = sum(a.size * a.dtype.itemsize for a in operands)
    return pl.pallas_call(
        kernel,
        out_shape=out_shape,
        in_specs=[IN_SMEM] + [IN_VMEM] * (len(operands) - 1),
        out_specs=IN_VMEM if single else [IN_VMEM] * len(out_shape),
        scratch_shapes=list(scratch),
        compiler_params=pltpu.CompilerParams(vmem_limit_bytes=grant * MIB),
        cost_estimate=pl.CostEstimate(flops=flops, bytes_accessed=moved, transcendentals=0),
    )(*operands)


TILES = (slice(0, 512), slice(512, 1024), slice(1024, 1152))
GRANT = 12
CUT_GRANT = 48


def terms_of(backs, weights, blocks, cols):
    total = None
    for i, block in enumerate(blocks):
        term = jnp.dot(block[...], weights[i % 2][backs[i // 2], :, cols], preferred_element_type=F32)
        total = term if total is None else total + term
    return total


def cut_kernel(at_ref, decoders_ref, out_ref, sems):
    target = at_ref[1]
    copies = [
        pltpu.make_async_copy(decoders_ref.at[0, jnp.maximum(target - back, 0)], out_ref.at[back], sems.at[back])
        for back in range(4)
    ]
    for copy in copies:
        copy.start()
    for back, copy in enumerate(copies):
        copy.wait()
        if back:

            @pl.when(target < back)
            def _(back=back):
                out_ref[back] = jnp.zeros_like(out_ref[back])


def cut(at, decoders):
    return pl.pallas_call(
        cut_kernel,
        out_shape=jax.ShapeDtypeStruct(decoders.shape[1:], BF),
        in_specs=[IN_SMEM, pl.BlockSpec(memory_space=pltpu.HBM)],
        out_specs=IN_VMEM,
        scratch_shapes=[pltpu.SemaphoreType.DMA((4,))],
        compiler_params=pltpu.CompilerParams(vmem_limit_bytes=CUT_GRANT * MIB),
        cost_estimate=pl.CostEstimate(flops=0, bytes_accessed=2 * decoders.size, transcendentals=0),
        name="cut",
    )(at, decoders)


def partial_kernel(backs, at_ref, *refs):
    weights, blocks, total_ref = refs[:2], refs[2:-1], refs[-1]
    for cols in TILES:
        total_ref[:, cols] = terms_of(backs, weights, blocks, cols)


def partial(at, weights, backs, blocks):
    rows, cols = blocks[0].shape[-2], weights[0].shape[2]
    return call(
        functools.partial(partial_kernel, backs),
        jax.ShapeDtypeStruct((rows, cols), F32),
        [at, *weights, *blocks], GRANT, flops=4 * len(backs) * rows * 512 * cols,
    )


def last_kernel(backs, has_base, at_ref, *refs):
    weights, refs = refs[:2], refs[2:]
    turned = refs[-1]
    self_ref, *away = refs[-5:-1]
    refs = refs[:-5]
    blocks = refs[has_base:]
    for cols in TILES:
        total = terms_of(backs, weights, blocks, cols)
        if has_base:
            total = total + refs[0][:, cols]
        turned[cols, :] = total.T
    for by in range(NX):
        owner = lax.rem(at_ref[2] + by, NX)
        for z in range(NZ):
            piece = turned[pl.ds(pl.multiple_of((z * NX + owner) * 72, 8), 72), :]
            if by == 0:
                self_ref[z] = piece
            else:
                away[by - 1][z] = piece.astype(BF)


def last(at, weights, base, backs, blocks):
    rows, cols = blocks[0].shape[-2], weights[0].shape[2]
    piece = (NZ, cols // (NX * NZ), rows)
    return call(
        functools.partial(last_kernel, backs, len(base)),
        [jax.ShapeDtypeStruct(piece, F32)] + [jax.ShapeDtypeStruct(piece, BF)] * 3,
        [at, *weights, *base, *blocks], GRANT,
        scratch=[pltpu.VMEM((cols, rows), F32)], flops=4 * len(backs) * rows * 512 * cols,
    )


def decode(at, weights, near, far):
    total = partial(at, weights, (0, 1, 3), near)
    return last(at, weights, [total], (2,), far)


def x_total(refs, z):
    self_ref, a_ref, b_ref, c_ref = refs
    return self_ref[z] + a_ref[z].astype(F32) + b_ref[z].astype(F32) + c_ref[z].astype(F32)


def x_sum_kernel(at_ref, *refs):
    for z in range(NZ):
        refs[-1][z] = x_total(refs[:-1], z)


def x_sum(at, kept, came):
    return call(x_sum_kernel, jax.ShapeDtypeStruct(kept.shape, F32), [at, kept, *came], 8)


def x_cut_kernel(at_ref, before_ref, *refs):
    for k, out_ref in enumerate(refs[4:]):
        z = at_ref[4] ^ k
        out_ref[0] = before_ref[z].astype(out_ref.dtype)
        out_ref[1] = x_total(refs[:4], z).astype(out_ref.dtype)


def x_cut(at, before, kept, came):
    shape = (2, *kept.shape[1:])
    out = [jax.ShapeDtypeStruct(shape, F32)] + [jax.ShapeDtypeStruct(shape, BF)] * 3
    return call(x_cut_kernel, out, [at, before, kept, *came], 8)


def z_sum_kernel(at_ref, kept_ref, a_ref, b_ref, c_ref, mine_ref, away_ref):
    total = kept_ref[...] + a_ref[...].astype(F32) + b_ref[...].astype(F32) + c_ref[...].astype(F32)
    low, high = total[:, :36], total[:, 36:]
    for core, (mine, away) in enumerate(((low, high), (high, low))):

        @pl.when(at_ref[0] == core)
        def _(mine=mine, away=away):
            mine_ref[...] = mine
            away_ref[...] = away


def z_sum(at, kept, came):
    out = [jax.ShapeDtypeStruct((2, 36, 256), F32)] * 2
    return call(z_sum_kernel, out, [at, kept, *came], 8)


def final_kernel(at_ref, mine_ref, came_ref, bias_ref, out_ref):
    for core in range(2):
        for dp in range(2):

            @pl.when((at_ref[0] == core) & (at_ref[3] == dp))
            def _(core=core, dp=dp):
                for ref, half in ((mine_ref, core), (came_ref, 1 - core)):
                    for block in range(2):
                        start = (dp ^ block) * 512 + half * 256
                        out_ref[:, start : start + 256] = (ref[block] + bias_ref[...]).astype(BF)


def finish(at, mine, came, bias):
    return call(final_kernel, jax.ShapeDtypeStruct((36, 1024), BF), [at, mine, came, bias], 8)


def per_device(resid, enc_weight, enc_bias, dec_weight, dec_bias, lengths):
    target, feat, dp = lax.axis_index("layer"), lax.axis_index("feat"), lax.axis_index("dp")
    core = feat % 2
    at = jnp.stack([core, target, feat // 2 % NX, dp, feat // 8]).astype(jnp.int32)
    valid = (jnp.arange(SEQ)[None, :] < lengths[:, None]).reshape(-1).astype(F32)
    pre = jnp.dot(resid[0], enc_weight[0], preferred_element_type=F32) + enc_bias
    acts = (jax.nn.relu(pre) * valid[:, None]).astype(BF).reshape(2, 256, 512)
    keep = lax.dynamic_index_in_dim(acts, core, 0, keepdims=False)
    send = lax.dynamic_index_in_dim(acts, 1 - core, 0, keepdims=False)
    across = lambda flip: [(d * 32 + f, (1 - d) * 32 + (f ^ flip)) for d in range(2) for f in range(32)]
    other_mine = lax.ppermute(keep, ("dp", "feat"), across(0))
    other_theirs = lax.ppermute(send, ("dp", "feat"), across(1))
    own_theirs = lax.ppermute(send, "feat", PARTNER)
    w_mine = cut(at, dec_weight)
    w_theirs = lax.ppermute(w_mine, "feat", PARTNER)
    weights = (w_mine, w_theirs)
    def shift(array, by):
        return lax.ppermute(array, "layer", ring(by))

    blocks = {}
    for name, mine, theirs in (("own", keep, own_theirs), ("other", other_mine, other_theirs)):
        up_mine, down_mine = shift(mine, 1), shift(mine, -1)
        up_theirs, down_theirs = shift(theirs, 1), shift(theirs, -1)
        onward = up_mine, down_theirs
        if name == "own":
            ahead = jnp.maximum(up_mine, 0)
            onward = ahead, jnp.maximum(down_theirs, 0)
        if name == "own":
            far = [shift(onward[0], 1), shift(onward[1], -1)]
        else:
            far = [shift(down_mine, -1), shift(up_theirs, 1)]
        near = [mine, theirs, up_mine, up_theirs, down_mine, down_theirs]
        blocks[name] = decode(at, weights, near, far)

    for name, (kept, *away) in blocks.items():
        came = []
        for by, piece in enumerate(away):
            came.append(lax.ppermute(piece, "feat", x_pairs(by + 1)))
        if name == "own":
            before = x_sum(at, kept, came)
        else:
            kept, *away = x_cut(at, before, kept, came)
    came = []
    for k in (2, 3, 1):
        came.append(lax.ppermute(away[k - 1], "feat", z_pairs(k)))
    mine, away = z_sum(at, kept, came)
    came = lax.ppermute(away, "feat", PARTNER)
    out = finish(at, mine, came, dec_bias.reshape(36, 1))
    return out.T[None]


def solution(mesh):
    in_specs = (
        P("layer", "dp", None),
        P("layer", None, "feat"),
        P("layer", "feat"),
        P("layer", None, "feat", "dp"),
        P("layer", ("dp", "feat")),
        P("dp"),
    )
    out_specs = P("layer", None, ("dp", "feat"))


    return jax.shard_map(per_device, mesh=mesh, in_specs=in_specs, out_specs=out_specs, check_vma=False)
```
